256 devices in a mesh: seq: 64 (over y, z, core), tp: 4 (over x).
Axes of the slice: x: 4, y: 4, z: 8, core: 2. Of those that a mesh axis runs over, the one named last changes fastest.
Arguments:
- tokens: bfloat16 [24576, 1024], P(('seq', 'tp')), may hold values from -6 to 6
- w_in: bfloat16 [3, 1024, 1024], P(None, None, 'tp'), may hold values from -0.1875 to 0.1875
- short_taps: float32 [3, 3, 1024], P(None, None, 'tp'), may hold values from -3.5 to 3.5
- skip_bias: float32 [2, 1024], P(None, 'tp'), may hold values from -4 to 4
- filter_spectra: float32 [2, 2, 128, 384, 1024], P(None, None, 'seq', None, 'tp'), may hold values from -6 to 6
- w_out: bfloat16 [1024, 1024], P('tp'), may hold values from -0.1875 to 0.1875
Outputs:
- mixed_out: bfloat16 [24576, 1024], P(('seq', 'tp'))
The draws below stay inside these ranges and needn't reach their ends.
All inputs are finite; a program needn't handle non-finite values.
Results may differ from the reference program's by a relative error of at most 0.007.
Values may be sent and summed in bfloat16 or wider, within the bound.
A program may use at most 64 MiB of HBM per device.

```python
import math
import jax
import jax.numpy as jnp
from jax import lax

D = 1024
ROWS_DEV = 384
SEQ_LEN = 24576
FREQ_BLOCKS = 128


def shard_levels(key, dims, cuts, low, largest):
    def one(axis_at, parts):
        heights = jax.random.uniform(jax.random.fold_in(jax.random.fold_in(key, 6), axis_at), (parts,), jnp.float32, low / len(cuts), largest / len(cuts))
        return jnp.repeat(jnp.exp(heights), dims[axis_at] // parts).reshape((-1,) + (1,) * (len(dims) - axis_at - 1))

    gain = one(*cuts[0])
    for cut in cuts[1:]:
        gain = gain * one(*cut)
    return gain


def bell_draw(key, shape, scale, most, split=(), kind=jnp.bfloat16):
    drawn = scale * jax.random.normal(key, shape, jnp.float32)
    if split:
        drawn = drawn * shard_levels(key, shape, split, -0.22, 0.18)
    return jnp.clip(drawn, -most, most).astype(kind)


def setup_inputs(seed: int = 0) -> dict:
    keys = jax.random.split(jax.random.key(seed), 7)
    return {
        "tokens": bell_draw(keys[0], (SEQ_LEN, D), 1.0, 6.0, ((0, 256),)),
        "w_in": bell_draw(keys[1], (3, D, D), D ** -0.5, 0.1875, ((2, 4),)),
        "short_taps": bell_draw(keys[2], (3, 3, D), 3 ** -0.5, 3.5, ((2, 4),), jnp.float32),
        "skip_bias": bell_draw(keys[3], (2, D), 1.0, 4.0, ((1, 4),), jnp.float32),
        "filter_spectra": bell_draw(keys[4], (2, 2, FREQ_BLOCKS, ROWS_DEV, D), 1.0, 6.0, ((2, 64), (4, 4)), jnp.float32),
        "w_out": bell_draw(keys[5], (D, D), D ** -0.5, 0.1875, ((0, 4),)),
    }


def reference(tokens, w_in, short_taps, skip_bias, filter_spectra, w_out):
    length, features = tokens.shape
    blocks = filter_spectra.shape[2]
    positions = filter_spectra.shape[3]
    padded_len = blocks * positions
    block_width = math.gcd(features, 128)

    def one_block(block_id):
        offset = block_id * block_width
        weights = lax.dynamic_slice_in_dim(w_in, offset, block_width, 2)
        tap_block = lax.dynamic_slice_in_dim(short_taps, offset, block_width, 2)
        bias_block = lax.dynamic_slice_in_dim(skip_bias, offset, block_width, 1)
        spectra = lax.dynamic_slice_in_dim(filter_spectra, offset, block_width, 4)
        rounded = jnp.stack([jnp.dot(tokens, weights[branch_id], preferred_element_type=jnp.float32) for branch_id in range(3)]).astype(jnp.bfloat16)
        projected = lax.optimization_barrier(rounded).astype(jnp.float32)
        padded = jnp.pad(projected, ((0, 0), (2, 0), (0, 0)))
        filtered = tap_block[:, 0, None, :] * projected + tap_block[:, 1, None, :] * padded[:, 1:-1] + tap_block[:, 2, None, :] * padded[:, :-2]
        natural = jnp.swapaxes(spectra, 2, 3).reshape(2, 2, padded_len, block_width)
        carried = filtered[0]
        for order_index in range(2):
            spectrum = jnp.fft.fft(carried, n=padded_len, axis=0)
            response = lax.complex(natural[order_index, 0], natural[order_index, 1])
            convolved = jnp.real(jnp.fft.ifft(spectrum * response, axis=0))[:length]
            carried = filtered[order_index + 1] * (convolved + bias_block[order_index] * carried)
        return carried.astype(jnp.bfloat16)

    pieces = lax.map(one_block, jnp.arange(features // block_width, dtype=jnp.int32))
    hidden = jnp.moveaxis(pieces, 0, 1).reshape(length, features)
    return jnp.dot(hidden, w_out, preferred_element_type=jnp.float32).astype(jnp.bfloat16)
```

```python
import math

import jax
import jax.numpy as jnp
import ml_dtypes
import numpy as np
from jax import lax
from jax.experimental import pallas as pl
from jax.experimental.pallas import tpu as pltpu
from jax.sharding import PartitionSpec as P

MESH = pl.DeviceIdType.MESH
BF = jnp.bfloat16
F32 = jnp.float32
SEQ, TP = 64, 4
ROWS, CH, OUT_ROWS = 384, 256, 96
RES = 128
NT = (((1,), (1,)), ((), ()))
NN = (((1,), (0,)), ((), ()))


def halves(table):
    high = table.astype(ml_dtypes.bfloat16)
    low = (table - high.astype(np.float64)).astype(ml_dtypes.bfloat16)
    return high, low


def tables():
    total = RES * ROWS
    line = np.arange(ROWS)
    inner = 2.0 * np.pi / ROWS * (np.outer(line, line) % ROWS)
    cos_hi, cos_lo = halves(np.cos(inner))
    sin_hi, sin_lo = halves(np.sin(inner))
    inner_table = np.stack([cos_hi, sin_hi, cos_lo, sin_lo])
    order = np.concatenate([2 * np.arange(SEQ), 2 * np.arange(SEQ) + 1])
    outer = 2.0 * np.pi / RES * (np.outer(order, np.arange(SEQ)) % RES)
    first = np.concatenate([np.cos(outer), -np.sin(outer)], axis=0)
    first_hi, first_lo = halves(first)
    first_table = np.concatenate([first_hi, first_hi, first_lo], axis=1)
    last = np.concatenate([np.cos(outer.T), -np.sin(outer.T)], axis=1) / total
    last_hi, last_lo = halves(last)
    last_table = np.concatenate([last_hi, last_hi, last_lo], axis=1)
    angle = -2.0 * np.pi / total * np.outer(order, line)
    twist = np.stack([np.cos(angle), np.sin(angle)]).astype(np.float32)
    pick = np.zeros((512, 512), ml_dtypes.bfloat16)
    for dest in range(SEQ):
        for slot in range(4):
            for low in range(2):
                pick[dest * 8 + slot * 2 + low, slot * 128 + low * 64 + dest] = 1
    return inner_table, first_table, last_table, twist, pick


def split(value):
    high = value.astype(BF)
    low = (value - high.astype(F32)).astype(BF)
    return high, low


def dot(a, b, dims=NN):
    return lax.dot_general(a, b, dims, preferred_element_type=F32)


def body(
    tok, w_in, taps_s, taps_v, bias_s, spec, w_out, inner_c, first_c, last_c, twist_c, pick_c,
    out,
    spec_v, w_in_v, inner_v, wmat, tg, wg, h_send, h_recv, f_send, f_recv, u_send, u_recv,
    wide, f2_v, halo, g_send, g_recv,
    load_sem, own_sem, tok_s, tok_r, wo_s, wo_r, h_s, h_r, f_s, f_r, halo_s, halo_r, u_s, u_r, g_s, g_r,
):
    me = lax.axis_index("seq")
    mx = lax.axis_index("tp")
    my_y = me // 16
    my_z = (me // 2) % 8
    my_c = me % 2

    def peer(i):
        return ((my_y + i // 16) % 4) * 16 + ((my_z + (i // 2) % 8) % 8) * 2 + (my_c + i % 2) % 2

    def loads(k):
        pairs = ((spec.at[0], spec_v.at[0]), (w_in, w_in_v), (spec.at[1], spec_v.at[1]), (inner_c, inner_v))
        return pltpu.make_async_copy(pairs[k][0], pairs[k][1], load_sem.at[k])

    for k in range(4):
        loads(k).start()

    barrier = pltpu.get_barrier_semaphore()

    def greet(i, carry):
        pl.semaphore_signal(barrier, inc=1, device_id={"seq": peer(i)}, device_id_type=MESH)
        return carry

    lax.fori_loop(1, SEQ, greet, 0)
    for t in range(1, TP):
        pl.semaphore_signal(barrier, inc=1, device_id={"tp": (mx + t) % TP}, device_id_type=MESH)
    pl.semaphore_wait(barrier, SEQ - 1 + TP - 1)

    def x_copy(src, dst, ssem, rsem, t):
        return pltpu.make_async_remote_copy(
            src, dst, ssem, rsem, device_id={"tp": (mx + t) % TP}, device_id_type=MESH
        )

    def own_copy(src, dst, k):
        return pltpu.make_async_copy(src, dst, own_sem.at[k])

    def all_wait(src_slice, dst_slice, ssem, rsem):
        pltpu.make_async_copy(src_slice, src_slice, ssem).wait()
        pltpu.make_async_copy(dst_slice, dst_slice, rsem).wait()

    for t in range(1, TP):
        x_copy(tok, tg.at[mx], tok_s, tok_r, t).start()
    own_copy(tok, tg.at[mx], 0).start()

    def spread(send, recv, ssem, rsem, k):
        def one(i, carry):
            to = peer(i)
            pltpu.make_async_remote_copy(
                send.at[to], recv.at[me], ssem, rsem, device_id={"seq": to}, device_id_type=MESH
            ).start()
            return carry

        lax.fori_loop(1, SEQ, one, 0)
        own_copy(send.at[me], recv.at[me], k).start()

    def gathered(send, recv, ssem, rsem, k):
        own_copy(send.at[me], recv.at[me], k).wait()
        pltpu.make_async_copy(recv.at[pl.ds(0, SEQ - 1)], recv.at[pl.ds(0, SEQ - 1)], rsem).wait()

    def sent(send, ssem):
        pltpu.make_async_copy(send.at[pl.ds(0, SEQ - 1)], send.at[pl.ds(0, SEQ - 1)], ssem).wait()

    def ship_filter(o, g):
        k = 2 * o + g
        lanes = slice(128 * g, 128 * g + 128)
        line = jnp.concatenate(
            [spec_v[o, ri, j, :, lanes].astype(BF) for ri in range(2) for j in range(2)], axis=1
        )
        turned = dot(pick_c[...], line, NT)
        h_send[k] = turned.reshape(SEQ, 8, ROWS).astype(BF)
        spread(h_send.at[k], h_recv.at[k], h_s.at[k], h_r.at[k], 4 + k)

    loads(0).wait()
    ship_filter(0, 0)
    ship_filter(0, 1)

    for t in range(1, TP):
        x_copy(w_out, wg.at[mx], wo_s, wo_r, t).start()
    own_copy(w_out, wg.at[mx], 1).start()

    loads(1).wait()
    own_copy(tok, tg.at[mx], 0).wait()
    pltpu.make_async_copy(tg.at[pl.ds(0, 3)], tg.at[pl.ds(0, 3)], tok_r).wait()
    rows = tg[...].reshape(ROWS, 1024)
    lines = [dot(rows, w_in_v[b]).astype(BF) for b in range(3)]
    turned = dot(pick_c[...], jnp.concatenate(lines[:2], axis=1), NT)
    f_send[...] = turned.reshape(SEQ, 8, ROWS).astype(BF)
    spread(f_send, f_recv, f_s, f_r, 2)
    f2_v[...] = lines[2]
    after = (me + 1) % SEQ
    edge = pltpu.make_async_remote_copy(
        f2_v.at[pl.ds(ROWS - 16, 16)], halo, halo_s, halo_r, device_id={"seq": after}, device_id_type=MESH
    )
    edge.start()

    loads(2).wait()
    ship_filter(1, 0)
    ship_filter(1, 1)

    loads(3).wait()
    for part in range(2):
        cos_t = inner_v[2 * part]
        sin_t = inner_v[2 * part + 1]
        wmat[part, 0:ROWS, 0:ROWS] = cos_t
        wmat[part, ROWS:, ROWS:] = cos_t
        wmat[part, ROWS:, 0:ROWS] = sin_t
        wmat[part, 0:ROWS, ROWS:] = -sin_t

    def thrice(value, dims):
        high, low = split(value)
        return dot(high, wmat[0], dims) + dot(low, wmat[0], dims) + dot(high, wmat[1], dims)

    def stacked(value):
        high, low = split(value)
        return jnp.concatenate([high, low, high], axis=0)

    def convolve(pair, k):
        wide[...] = h_recv[k].astype(F32)
        z = dot(first_c[...], stacked(jnp.concatenate(pair, axis=1)))
        tr, ti = twist_c[0], twist_c[1]
        blocks = []
        for low in range(2):
            cols = slice(ROWS * low, ROWS * low + ROWS)
            zr, zi = z[:RES, cols], z[RES:, cols]
            blocks.append(jnp.concatenate([zr * tr - zi * ti, zr * ti + zi * tr], axis=1))
        x = thrice(jnp.concatenate(blocks, axis=0), NN)
        blocks = []
        for low in range(2):
            for j in range(2):
                at = low * RES + j * SEQ
                xr, xi = x[at : at + SEQ, :ROWS], x[at : at + SEQ, ROWS:]
                hr = wide[:, j * 2 + low, :]
                hi = wide[:, (2 + j) * 2 + low, :]
                blocks.append(jnp.concatenate([xr * hr - xi * hi, xr * hi + xi * hr], axis=1))
        v = thrice(jnp.concatenate(blocks, axis=0), NT)
        real, imag = [], []
        for low in range(2):
            vr, vi = v[RES * low : RES * low + RES, :ROWS], v[RES * low : RES * low + RES, ROWS:]
            real.append(vr * tr + vi * ti)
            imag.append(vi * tr - vr * ti)
        rhs = jnp.concatenate([jnp.concatenate(real, axis=1), jnp.concatenate(imag, axis=1)], axis=0)
        y = dot(last_c[...], stacked(rhs))
        return [y[:, :ROWS], y[:, ROWS:]]

    at_row = lax.broadcasted_iota(jnp.int32, (SEQ, ROWS), 0)
    at_col = lax.broadcasted_iota(jnp.int32, (SEQ, ROWS), 1)

    def delayed(x, by):
        turned = pltpu.roll(x, by, 1)
        fix = jnp.where(at_row == 0, 0.0, pltpu.roll(turned, 1, 0))
        return jnp.where(at_col < by, fix, turned)

    def filtered(b, i):
        x = wide[:, b * 4 + i, :]
        col = 64 * i + me
        return taps_s[b, 0, col] * x + taps_s[b, 1, col] * delayed(x, 1) + taps_s[b, 2, col] * delayed(x, 2)

    gathered(f_send, f_recv, f_s, f_r, 2)
    wide[...] = f_recv[...].astype(F32)
    values = [filtered(0, i) for i in range(4)]
    gates = [filtered(1, i) for i in range(4)]
    carried = []
    for g in range(2):
        gathered(h_send.at[g], h_recv.at[g], h_s.at[g], h_r.at[g], 4 + g)
        ys = convolve(values[2 * g : 2 * g + 2], g)
        for low in range(2):
            i = 2 * g + low
            carried.append(gates[i] * (ys[low] + bias_s[0, 64 * i + me] * values[i]))
    ends = []
    for g in range(2):
        k = 2 + g
        gathered(h_send.at[k], h_recv.at[k], h_s.at[k], h_r.at[k], 4 + k)
        ys = convolve(carried[2 * g : 2 * g + 2], k)
        for low in range(2):
            i = 2 * g + low
            ends.append(ys[low] + bias_s[1, 64 * i + me] * carried[i])
    for i in range(4):
        wide[:, i, :] = ends[i]
    u_send[...] = wide[:, 0:4, :].astype(BF)
    spread(u_send, u_recv, u_s, u_r, 3)

    edge.wait()
    x = f2_v[...].astype(F32)
    edge_rows = jnp.where(me > 0, halo[...].astype(F32), 0.0)
    at = lax.broadcasted_iota(jnp.int32, (ROWS, CH), 0)
    one = jnp.where(at == 0, edge_rows[15:16], pltpu.roll(x, 1, 0))
    two = jnp.where(at == 0, edge_rows[14:15], jnp.where(at == 1, edge_rows[15:16], pltpu.roll(x, 2, 0)))
    gate = taps_v[2, 0:1, :] * x + taps_v[2, 1:2, :] * one + taps_v[2, 2:3, :] * two

    gathered(u_send, u_recv, u_s, u_r, 3)
    wide[:, 0:4, :] = u_recv[...].astype(F32)
    turned = jnp.concatenate([wide[:, i, :] for i in range(4)], axis=0).T
    g_send[...] = (gate * turned).astype(BF).reshape(TP, OUT_ROWS, CH)
    for t in range(1, TP):
        x_copy(g_send.at[(mx + t) % TP], g_recv.at[mx], g_s, g_r, t).start()
    own_copy(g_send.at[mx], g_recv.at[mx], 8).start()
    own_copy(w_out, wg.at[mx], 1).wait()
    pltpu.make_async_copy(wg.at[pl.ds(0, 3)], wg.at[pl.ds(0, 3)], wo_r).wait()
    own_copy(g_send.at[mx], g_recv.at[mx], 8).wait()
    pltpu.make_async_copy(g_recv.at[pl.ds(0, 3)], g_recv.at[pl.ds(0, 3)], g_r).wait()
    total = dot(g_recv[0], wg[0])
    for t in range(1, TP):
        total = total + dot(g_recv[t], wg[t])
    out[...] = total.astype(BF)

    pltpu.make_async_copy(tg.at[pl.ds(0, 3)], tg.at[pl.ds(0, 3)], tok_s).wait()
    pltpu.make_async_copy(wg.at[pl.ds(0, 3)], wg.at[pl.ds(0, 3)], wo_s).wait()
    for k in range(4):
        sent(h_send.at[k], h_s.at[k])
    sent(f_send, f_s)
    sent(u_send, u_s)
    pltpu.make_async_copy(g_send.at[pl.ds(0, 3)], g_send.at[pl.ds(0, 3)], g_s).wait()


def local(tokens, w_in, short_taps, skip_bias, filter_spectra, w_out):
    inner_table, first_table, last_table, twist, pick = tables()
    vmem = pl.BlockSpec(memory_space=pltpu.VMEM)
    smem = pl.BlockSpec(memory_space=pltpu.SMEM)
    hbm = pl.BlockSpec(memory_space=pl.ANY)
    dma = pltpu.SemaphoreType.DMA
    return pl.pallas_call(
        body,
        out_shape=jax.ShapeDtypeStruct((OUT_ROWS, 1024), BF),
        in_specs=[vmem, hbm, smem, vmem, smem, hbm, hbm, hbm, vmem, vmem, vmem, vmem],
        out_specs=vmem,
        scratch_shapes=[
            pltpu.VMEM((2, 2, 2, ROWS, CH), F32),
            pltpu.VMEM((3, 1024, CH), BF),
            pltpu.VMEM((4, ROWS, ROWS), BF),
            pltpu.VMEM((2, 2 * ROWS, 2 * ROWS), BF),
            pltpu.VMEM((TP, OUT_ROWS, 1024), BF),
            pltpu.VMEM((TP, CH, 1024), BF),
            pltpu.VMEM((4, SEQ, 8, ROWS), BF),
            pltpu.VMEM((4, SEQ, 8, ROWS), BF),
            pltpu.VMEM((SEQ, 8, ROWS), BF),
            pltpu.VMEM((SEQ, 8, ROWS), BF),
            pltpu.VMEM((SEQ, 4, ROWS), BF),
            pltpu.VMEM((SEQ, 4, ROWS), BF),
            pltpu.VMEM((SEQ, 8, ROWS), F32),
            pltpu.VMEM((ROWS, CH), BF),
            pltpu.VMEM((16, CH), BF),
            pltpu.VMEM((TP, OUT_ROWS, CH), BF),
            pltpu.VMEM((TP, OUT_ROWS, CH), BF),
            dma((4,)),
            dma((9,)),
            dma, dma, dma, dma,
            dma((4,)),
            dma((4,)),
            dma, dma, dma, dma, dma, dma, dma, dma,
        ],
        compiler_params=pltpu.CompilerParams(
            collective_id=0, has_side_effects=True, vmem_limit_bytes=60 * 1024 * 1024
        ),
    )(
        tokens, w_in, short_taps, short_taps, skip_bias, filter_spectra, w_out,
        jnp.asarray(inner_table), jnp.asarray(first_table), jnp.asarray(last_table),
        jnp.asarray(twist), jnp.asarray(pick),
    )


def solution(mesh):
    in_specs = (
        P(("seq", "tp"), None),
        P(None, None, "tp"),
        P(None, None, "tp"),
        P(None, "tp"),
        P(None, None, "seq", None, "tp"),
        P("tp", None),
    )
    out_specs = P(("seq", "tp"), None)
    return jax.shard_map(local, mesh=mesh, in_specs=in_specs, out_specs=out_specs, check_vma=False)
```

```python
import math

import jax
import jax.numpy as jnp
import ml_dtypes
import numpy as np
from jax import lax
from jax.experimental import pallas as pl
from jax.experimental.pallas import tpu as pltpu
from jax.sharding import PartitionSpec as P

MESH = pl.DeviceIdType.MESH
BF = jnp.bfloat16
F32 = jnp.float32
SEQ, TP = 64, 4
ROWS, CH, OUT_ROWS = 384, 256, 96
RES = 128
NT = (((1,), (1,)), ((), ()))
NN = (((1,), (0,)), ((), ()))


def halves(table):
    high = table.astype(ml_dtypes.bfloat16)
    low = (table - high.astype(np.float64)).astype(ml_dtypes.bfloat16)
    return high, low


def tables():
    total = RES * ROWS
    line = np.arange(ROWS)
    inner = 2.0 * np.pi / ROWS * (np.outer(line, line) % ROWS)
    cos_hi, cos_lo = halves(np.cos(inner))
    sin_hi, sin_lo = halves(np.sin(inner))
    inner_table = np.stack([cos_hi, sin_hi, cos_lo, sin_lo])
    order = np.concatenate([2 * np.arange(SEQ), 2 * np.arange(SEQ) + 1])
    outer = 2.0 * np.pi / RES * (np.outer(order, np.arange(SEQ)) % RES)
    first = np.concatenate([np.cos(outer), -np.sin(outer)], axis=0)
    first_hi, first_lo = halves(first)
    first_table = np.concatenate([first_hi, first_hi, first_lo], axis=1)
    last = np.concatenate([np.cos(outer.T), -np.sin(outer.T)], axis=1) / total
    last_hi, last_lo = halves(last)
    last_table = np.concatenate([last_hi, last_hi, last_lo], axis=1)
    angle = -2.0 * np.pi / total * np.outer(order, line)
    twist = np.stack([np.cos(angle), np.sin(angle)]).astype(np.float32)
    pick = np.zeros((512, 512), ml_dtypes.bfloat16)
    for dest in range(SEQ):
        for slot in range(4):
            for low in range(2):
                pick[dest * 8 + slot * 2 + low, slot * 128 + low * 64 + dest] = 1
    return inner_table, first_table, last_table, twist, pick


def split(value):
    high = value.astype(BF)
    low = (value - high.astype(F32)).astype(BF)
    return high, low


def dot(a, b, dims=NN):
    return lax.dot_general(a, b, dims, preferred_element_type=F32)


def body(
    tok, w_in, taps_h, bias_h, spec, w_out, inner_h, first_h, last_h, twist_h, pick_h,
    out,
    taps_s, bias_s, taps_v, first_c, last_c, twist_c, pick_c, spec_v, w_in_v, inner_v, wmat, tg, wg, h_send, h_recv, f_send, f_recv, u_send, u_recv,
    wide, f2_v, halo, gate_v, g_send, g_recv,
    load_sem, own_sem, tok_s, tok_r, wo_s, wo_r, h_s, h_r, f_s, f_r, halo_s, halo_r, u_s, u_r, g_s, g_r,
):
    me = lax.axis_index("seq")
    mx = lax.axis_index("tp")

    def peer(i):
        to = me + i
        return jnp.where(to >= SEQ, to - SEQ, to)

    barrier = pltpu.get_barrier_semaphore()

    def greet(i, carry):
        pl.semaphore_signal(barrier, inc=1, device_id={"seq": peer(i)}, device_id_type=MESH)
        return carry

    lax.fori_loop(1, SEQ, greet, 0)
    for t in range(1, TP):
        pl.semaphore_signal(barrier, inc=1, device_id={"tp": (mx + t) % TP}, device_id_type=MESH)

    def loads(k):
        pairs = (
            (spec.at[0], spec_v.at[0]), (pick_h, pick_c), (w_in, w_in_v), (spec.at[1], spec_v.at[1]),
            (inner_h, inner_v), (first_h, first_c), (twist_h, twist_c), (last_h, last_c),
            (taps_h, taps_v), (taps_h, taps_s), (bias_h, bias_s),
        )
        return pltpu.make_async_copy(pairs[k][0], pairs[k][1], load_sem.at[k])

    for k in range(11):
        loads(k).start()

    def x_copy(src, dst, ssem, rsem, t):
        return pltpu.make_async_remote_copy(
            src, dst, ssem, rsem, device_id={"tp": (mx + t) % TP}, device_id_type=MESH
        )

    def own_copy(src, dst, k):
        return pltpu.make_async_copy(src, dst, own_sem.at[k])

    def all_wait(src_slice, dst_slice, ssem, rsem):
        pltpu.make_async_copy(src_slice, src_slice, ssem).wait()
        pltpu.make_async_copy(dst_slice, dst_slice, rsem).wait()

    def spread(send, recv, ssem, rsem, k):
        def one(i, carry):
            to = peer(i)
            pltpu.make_async_remote_copy(
                send.at[to], recv.at[me], ssem, rsem, device_id={"seq": to}, device_id_type=MESH
            ).start()
            return carry

        lax.fori_loop(1, SEQ, one, 0)
        own_copy(send.at[me], recv.at[me], k).start()

    def gathered(send, recv, ssem, rsem, k):
        own_copy(send.at[me], recv.at[me], k).wait()
        pltpu.make_async_copy(recv.at[pl.ds(0, SEQ - 1)], recv.at[pl.ds(0, SEQ - 1)], rsem).wait()

    def sent(send, ssem):
        pltpu.make_async_copy(send.at[pl.ds(0, SEQ - 1)], send.at[pl.ds(0, SEQ - 1)], ssem).wait()

    def turn_filter(o, g):
        k = 2 * o + g
        lanes = slice(128 * g, 128 * g + 128)
        line = jnp.concatenate(
            [spec_v[o, ri, j, :, lanes].astype(BF) for ri in range(2) for j in range(2)], axis=1
        )
        turned = dot(pick_c[...], line, NT)
        h_send[k] = turned.reshape(SEQ, 8, ROWS).astype(BF)

    def ship_filter(k):
        spread(h_send.at[k], h_recv.at[k], h_s.at[k], h_r.at[k], 4 + k)

    loads(0).wait()
    loads(1).wait()
    turn_filter(0, 0)
    turn_filter(0, 1)
    pl.semaphore_wait(barrier, SEQ - 1 + TP - 1)
    for t in range(1, TP):
        x_copy(tok, tg.at[mx], tok_s, tok_r, t).start()
    own_copy(tok, tg.at[mx], 0).start()
    ship_filter(0)
    ship_filter(1)

    for t in range(1, TP):
        x_copy(w_out, wg.at[mx], wo_s, wo_r, t).start()
    own_copy(w_out, wg.at[mx], 1).start()

    loads(2).wait()
    own_copy(tok, tg.at[mx], 0).wait()
    pltpu.make_async_copy(tg.at[pl.ds(0, 3)], tg.at[pl.ds(0, 3)], tok_r).wait()
    rows = tg[...].reshape(ROWS, 1024)
    lines = [dot(rows, w_in_v[b]).astype(BF) for b in range(3)]
    turned = dot(pick_c[...], jnp.concatenate(lines[:2], axis=1), NT)
    f_send[...] = turned.reshape(SEQ, 8, ROWS).astype(BF)
    spread(f_send, f_recv, f_s, f_r, 2)
    f2_v[...] = lines[2]
    after = (me + 1) % SEQ
    edge = pltpu.make_async_remote_copy(
        f2_v.at[pl.ds(ROWS - 16, 16)], halo, halo_s, halo_r, device_id={"seq": after}, device_id_type=MESH
    )
    edge.start()

    loads(3).wait()
    for g in range(2):
        turn_filter(1, g)
        ship_filter(2 + g)

    for k in range(4, 11):
        loads(k).wait()
    for part in range(2):
        cos_t = inner_v[2 * part]
        sin_t = inner_v[2 * part + 1]
        wmat[part, 0:ROWS, 0:ROWS] = cos_t
        wmat[part, ROWS:, ROWS:] = cos_t
        wmat[part, ROWS:, 0:ROWS] = sin_t
        wmat[part, 0:ROWS, ROWS:] = -sin_t

    def thrice(value, dims):
        high, low = split(value)
        return dot(high, wmat[0], dims) + dot(low, wmat[0], dims) + dot(high, wmat[1], dims)

    def stacked(value):
        high, low = split(value)
        return jnp.concatenate([high, low, high], axis=0)

    tr, ti = twist_c[0], twist_c[1]

    def forward(pair):
        z = dot(first_c[...], stacked(jnp.concatenate(pair, axis=1)))
        blocks = []
        for low in range(2):
            cols = slice(ROWS * low, ROWS * low + ROWS)
            zr, zi = z[:RES, cols], z[RES:, cols]
            blocks.append(jnp.concatenate([zr * tr - zi * ti, zr * ti + zi * tr], axis=1))
        return thrice(jnp.concatenate(blocks, axis=0), NN)

    def inverse(x, k):
        gathered(h_send.at[k], h_recv.at[k], h_s.at[k], h_r.at[k], 4 + k)
        wide[...] = h_recv[k].astype(F32)
        blocks = []
        for low in range(2):
            for j in range(2):
                at = low * RES + j * SEQ
                xr, xi = x[at : at + SEQ, :ROWS], x[at : at + SEQ, ROWS:]
                hr = wide[:, j * 2 + low, :]
                hi = wide[:, (2 + j) * 2 + low, :]
                blocks.append(jnp.concatenate([xr * hr - xi * hi, xr * hi + xi * hr], axis=1))
        v = thrice(jnp.concatenate(blocks, axis=0), NT)
        real, imag = [], []
        for low in range(2):
            vr, vi = v[RES * low : RES * low + RES, :ROWS], v[RES * low : RES * low + RES, ROWS:]
            real.append(vr * tr + vi * ti)
            imag.append(vi * tr - vr * ti)
        rhs = jnp.concatenate([jnp.concatenate(real, axis=1), jnp.concatenate(imag, axis=1)], axis=0)
        y = dot(last_c[...], stacked(rhs))
        return [y[:, :ROWS], y[:, ROWS:]]

    at_row = lax.broadcasted_iota(jnp.int32, (SEQ, ROWS), 0)
    at_col = lax.broadcasted_iota(jnp.int32, (SEQ, ROWS), 1)

    def delayed(x, by):
        turned = pltpu.roll(x, by, 1)
        fix = jnp.where(at_row == 0, 0.0, pltpu.roll(turned, 1, 0))
        return jnp.where(at_col < by, fix, turned)

    def filtered(b, i):
        x = wide[:, b * 4 + i, :]
        col = 64 * i + me
        return taps_s[b, 0, col] * x + taps_s[b, 1, col] * delayed(x, 1) + taps_s[b, 2, col] * delayed(x, 2)

    gathered(f_send, f_recv, f_s, f_r, 2)
    wide[...] = f_recv[...].astype(F32)
    values = [filtered(0, i) for i in range(4)]
    gates = [filtered(1, i) for i in range(4)]
    spectra = [forward(values[2 * g : 2 * g + 2]) for g in range(2)]
    carried = []
    for g in range(2):
        ys = inverse(spectra[g], g)
        for low in range(2):
            i = 2 * g + low
            carried.append(gates[i] * (ys[low] + bias_s[0, 64 * i + me] * values[i]))
        spectra[g] = forward(carried[2 * g : 2 * g + 2])

    edge.wait()
    x = f2_v[...].astype(F32)
    edge_rows = jnp.where(me > 0, halo[...].astype(F32), 0.0)
    at = lax.broadcasted_iota(jnp.int32, (ROWS, CH), 0)
    one = jnp.where(at == 0, edge_rows[15:16], pltpu.roll(x, 1, 0))
    two = jnp.where(at == 0, edge_rows[14:15], jnp.where(at == 1, edge_rows[15:16], pltpu.roll(x, 2, 0)))
    gate_v[...] = taps_v[2, 0:1, :] * x + taps_v[2, 1:2, :] * one + taps_v[2, 2:3, :] * two

    for g in range(2):
        ys = inverse(spectra[g], 2 + g)
        for low in range(2):
            i = 2 * g + low
            wide[:, low, :] = ys[low] + bias_s[1, 64 * i + me] * carried[i]
        u_send[g] = wide[:, 0:2, :].astype(BF)
        spread(u_send.at[g], u_recv.at[g], u_s.at[g], u_r.at[g], 8 + g)

    for g in range(2):
        gathered(u_send.at[g], u_recv.at[g], u_s.at[g], u_r.at[g], 8 + g)
        wide[:, 0:2, :] = u_recv[g].astype(F32)
        turned = jnp.concatenate([wide[:, low, :] for low in range(2)], axis=0).T
        lanes = slice(128 * g, 128 * g + 128)
        g_send[g] = (gate_v[:, lanes] * turned).astype(BF).reshape(TP, OUT_ROWS, 128)
        for t in range(1, TP):
            x_copy(g_send.at[g, (mx + t) % TP], g_recv.at[g, mx], g_s.at[g], g_r.at[g], t).start()
        own_copy(g_send.at[g, mx], g_recv.at[g, mx], 10 + g).start()
    own_copy(w_out, wg.at[mx], 1).wait()
    pltpu.make_async_copy(wg.at[pl.ds(0, 3)], wg.at[pl.ds(0, 3)], wo_r).wait()
    parts = []
    for g in range(2):
        own_copy(g_send.at[g, mx], g_recv.at[g, mx], 10 + g).wait()
        pltpu.make_async_copy(g_recv.at[g, pl.ds(0, 3)], g_recv.at[g, pl.ds(0, 3)], g_r.at[g]).wait()
        line = jnp.concatenate([g_recv[g, t] for t in range(TP)], axis=1)
        parts.append(dot(line, wg[:, g].reshape(512, 1024)))
    out[...] = (parts[0] + parts[1]).astype(BF)

    pltpu.make_async_copy(tg.at[pl.ds(0, 3)], tg.at[pl.ds(0, 3)], tok_s).wait()
    pltpu.make_async_copy(wg.at[pl.ds(0, 3)], wg.at[pl.ds(0, 3)], wo_s).wait()
    for k in range(4):
        sent(h_send.at[k], h_s.at[k])
    sent(f_send, f_s)
    for g in range(2):
        sent(u_send.at[g], u_s.at[g])
        pltpu.make_async_copy(g_send.at[g, pl.ds(0, 3)], g_send.at[g, pl.ds(0, 3)], g_s.at[g]).wait()


def local(tokens, w_in, short_taps, skip_bias, filter_spectra, w_out):
    inner_table, first_table, last_table, twist, pick = tables()
    vmem = pl.BlockSpec(memory_space=pltpu.VMEM)
    hbm = pl.BlockSpec(memory_space=pl.ANY)
    dma = pltpu.SemaphoreType.DMA
    return pl.pallas_call(
        body,
        out_shape=jax.ShapeDtypeStruct((OUT_ROWS, 1024), BF),
        in_specs=[hbm] * 11,
        out_specs=vmem,
        scratch_shapes=[
            pltpu.SMEM((3, 3, CH), F32),
            pltpu.SMEM((2, CH), F32),
            pltpu.VMEM((3, 3, CH), F32),
            pltpu.VMEM((2 * RES, 3 * SEQ), BF),
            pltpu.VMEM((SEQ, 6 * RES), BF),
            pltpu.VMEM((2, RES, ROWS), F32),
            pltpu.VMEM((512, 512), BF),
            pltpu.VMEM((2, 2, 2, ROWS, CH), F32),
            pltpu.VMEM((3, 1024, CH), BF),
            pltpu.VMEM((4, ROWS, ROWS), BF),
            pltpu.VMEM((2, 2 * ROWS, 2 * ROWS), BF),
            pltpu.VMEM((TP, OUT_ROWS, 1024), BF),
            pltpu.VMEM((TP, 2, 128, 1024), BF),
            pltpu.VMEM((4, SEQ, 8, ROWS), BF),
            pltpu.VMEM((4, SEQ, 8, ROWS), BF),
            pltpu.VMEM((SEQ, 8, ROWS), BF),
            pltpu.VMEM((SEQ, 8, ROWS), BF),
            pltpu.VMEM((2, SEQ, 2, ROWS), BF),
            pltpu.VMEM((2, SEQ, 2, ROWS), BF),
            pltpu.VMEM((SEQ, 8, ROWS), F32),
            pltpu.VMEM((ROWS, CH), BF),
            pltpu.VMEM((16, CH), BF),
            pltpu.VMEM((ROWS, CH), F32),
            pltpu.VMEM((2, TP, OUT_ROWS, 128), BF),
            pltpu.VMEM((2, TP, OUT_ROWS, 128), BF),
            dma((11,)),
            dma((12,)),
            dma, dma, dma, dma,
            dma((4,)),
            dma((4,)),
            dma, dma, dma, dma, dma((2,)), dma((2,)), dma((2,)), dma((2,)),
        ],
        compiler_params=pltpu.CompilerParams(
            collective_id=0, has_side_effects=True, vmem_limit_bytes=60 * 1024 * 1024
        ),
    )(
        tokens, w_in, short_taps, skip_bias, filter_spectra, w_out.reshape(2, 128, 1024),
        jnp.asarray(inner_table), jnp.asarray(first_table), jnp.asarray(last_table),
        jnp.asarray(twist), jnp.asarray(pick),
    )


def solution(mesh):
    in_specs = (
        P(("seq", "tp"), None),
        P(None, None, "tp"),
        P(None, None, "tp"),
        P(None, "tp"),
        P(None, None, "seq", None, "tp"),
        P("tp", None),
    )
    out_specs = P(("seq", "tp"), None)
    return jax.shard_map(local, mesh=mesh, in_specs=in_specs, out_specs=out_specs, check_vma=False)
```

```python
import math

import jax
import jax.numpy as jnp
import ml_dtypes
import numpy as np
from jax import lax
from jax.experimental import pallas as pl
from jax.experimental.pallas import tpu as pltpu
from jax.sharding import PartitionSpec as P

MESH = pl.DeviceIdType.MESH
BF = jnp.bfloat16
F32 = jnp.float32
SEQ, TP = 64, 4
ROWS, CH, OUT_ROWS = 384, 256, 96
RES = 128
NT = (((1,), (1,)), ((), ()))
NN = (((1,), (0,)), ((), ()))


def halves(table):
    high = table.astype(ml_dtypes.bfloat16)
    low = (table - high.astype(np.float64)).astype(ml_dtypes.bfloat16)
    return high, low


def tables():
    total = RES * ROWS
    line = np.arange(ROWS)
    inner = 2.0 * np.pi / ROWS * (np.outer(line, line) % ROWS)
    cos_hi, cos_lo = halves(np.cos(inner))
    sin_hi, sin_lo = halves(np.sin(inner))
    inner_table = np.stack([cos_hi, sin_hi, cos_lo, sin_lo])
    order = np.concatenate([2 * np.arange(SEQ), 2 * np.arange(SEQ) + 1])
    outer = 2.0 * np.pi / RES * (np.outer(order, np.arange(SEQ)) % RES)
    first = np.concatenate([np.cos(outer), -np.sin(outer)], axis=0)
    first_hi, first_lo = halves(first)
    first_table = np.concatenate([first_hi, first_hi, first_lo], axis=1)
    last = np.concatenate([np.cos(outer.T), -np.sin(outer.T)], axis=1) / total
    last_hi, last_lo = halves(last)
    last_table = np.concatenate([last_hi, last_hi, last_lo], axis=1)
    angle = -2.0 * np.pi / total * np.outer(order, line)
    twist = np.stack([np.cos(angle), np.sin(angle)]).astype(np.float32)
    pick = np.zeros((512, 512), ml_dtypes.bfloat16)
    for dest in range(SEQ):
        for slot in range(4):
            for low in range(2):
                pick[dest * 8 + slot * 2 + low, slot * 128 + low * 64 + dest] = 1
    return inner_table, first_table, last_table, twist, pick


def split(value):
    high = value.astype(BF)
    low = (value - high.astype(F32)).astype(BF)
    return high, low


def dot(a, b, dims=NN):
    return lax.dot_general(a, b, dims, preferred_element_type=F32)


def body(
    tok, w_in, taps_h, bias_h, spec, w_out, inner_h, first_h, last_h, twist_h, pick_h,
    out,
    taps_s, bias_s, taps_v, first_c, last_c, twist_c, pick_c, spec_v, w_in_v, inner_v, wmat, tg, wg, h_send, h_recv, f_send, f_recv, u_send, u_recv,
    wide, f2_v, halo, gate_v, g_send, g_recv,
    load_sem, own_sem, tok_s, tok_r, wo_s, wo_r, h_s, h_r, f_s, f_r, halo_s, halo_r, u_s, u_r, g_s, g_r,
):
    me = lax.axis_index("seq")
    mx = lax.axis_index("tp")

    def peer(i):
        to = me + i
        return jnp.where(to >= SEQ, to - SEQ, to)

    barrier = pltpu.get_barrier_semaphore()

    def greet(i, carry):
        pl.semaphore_signal(barrier, inc=1, device_id={"seq": peer(i)}, device_id_type=MESH)
        return carry

    lax.fori_loop(1, SEQ, greet, 0, unroll=7)
    for t in range(1, TP):
        pl.semaphore_signal(barrier, inc=1, device_id={"tp": (mx + t) % TP}, device_id_type=MESH)

    def half(ref, o, g):
        return ref.at[o, :, :, :, pl.ds(128 * g, 128)]

    def loads(k):
        pairs = (
            (half(spec, 0, 0), half(spec_v, 0, 0)), (pick_h, pick_c), (half(spec, 0, 1), half(spec_v, 0, 1)),
            (w_in, w_in_v), (half(spec, 1, 0), half(spec_v, 1, 0)), (half(spec, 1, 1), half(spec_v, 1, 1)),
            (inner_h, inner_v), (first_h, first_c), (twist_h, twist_c), (last_h, last_c),
            (taps_h, taps_v), (taps_h, taps_s), (bias_h, bias_s),
        )
        return pltpu.make_async_copy(pairs[k][0], pairs[k][1], load_sem.at[k])

    for k in range(13):
        loads(k).start()

    def x_copy(src, dst, ssem, rsem, t):
        return pltpu.make_async_remote_copy(
            src, dst, ssem, rsem, device_id={"tp": (mx + t) % TP}, device_id_type=MESH
        )

    def own_copy(src, dst, k):
        return pltpu.make_async_copy(src, dst, own_sem.at[k])

    def all_wait(src_slice, dst_slice, ssem, rsem):
        pltpu.make_async_copy(src_slice, src_slice, ssem).wait()
        pltpu.make_async_copy(dst_slice, dst_slice, rsem).wait()

    def spread(send, recv, ssem, rsem, k):
        def one(i, carry):
            to = peer(i)
            pltpu.make_async_remote_copy(
                send.at[to], recv.at[me], ssem, rsem, device_id={"seq": to}, device_id_type=MESH
            ).start()
            return carry

        lax.fori_loop(1, SEQ, one, 0, unroll=7)
        own_copy(send.at[me], recv.at[me], k).start()

    def gathered(send, recv, ssem, rsem, k):
        own_copy(send.at[me], recv.at[me], k).wait()
        pltpu.make_async_copy(recv.at[pl.ds(0, SEQ - 1)], recv.at[pl.ds(0, SEQ - 1)], rsem).wait()

    def sent(send, ssem):
        pltpu.make_async_copy(send.at[pl.ds(0, SEQ - 1)], send.at[pl.ds(0, SEQ - 1)], ssem).wait()

    def turn_filter(o, g):
        k = 2 * o + g
        lanes = slice(128 * g, 128 * g + 128)
        line = jnp.concatenate(
            [spec_v[o, ri, j, :, lanes].astype(BF) for ri in range(2) for j in range(2)], axis=1
        )
        turned = dot(pick_c[...], line, NT)
        h_send[k] = turned.reshape(SEQ, 8, ROWS).astype(BF)

    def ship_filter(k):
        spread(h_send.at[k], h_recv.at[k], h_s.at[k], h_r.at[k], 4 + k)

    loads(0).wait()
    loads(1).wait()
    turn_filter(0, 0)
    pl.semaphore_wait(barrier, SEQ - 1 + TP - 1)
    for t in range(1, TP):
        x_copy(tok, tg.at[mx], tok_s, tok_r, t).start()
    own_copy(tok, tg.at[mx], 0).start()
    ship_filter(0)
    loads(2).wait()
    turn_filter(0, 1)
    ship_filter(1)

    for t in range(1, TP):
        x_copy(w_out, wg.at[mx], wo_s, wo_r, t).start()
    own_copy(w_out, wg.at[mx], 1).start()

    loads(3).wait()
    own_copy(tok, tg.at[mx], 0).wait()
    pltpu.make_async_copy(tg.at[pl.ds(0, 3)], tg.at[pl.ds(0, 3)], tok_r).wait()
    rows = tg[...].reshape(ROWS, 1024)
    lines = [dot(rows, w_in_v[b]).astype(BF) for b in range(3)]
    turned = dot(pick_c[...], jnp.concatenate(lines[:2], axis=1), NT)
    f_send[...] = turned.reshape(SEQ, 8, ROWS).astype(BF)
    spread(f_send, f_recv, f_s, f_r, 2)
    f2_v[...] = lines[2]
    after = (me + 1) % SEQ
    edge = pltpu.make_async_remote_copy(
        f2_v.at[pl.ds(ROWS - 16, 16)], halo, halo_s, halo_r, device_id={"seq": after}, device_id_type=MESH
    )
    edge.start()

    for g in range(2):
        loads(4 + g).wait()
        turn_filter(1, g)
        ship_filter(2 + g)

    for k in range(6, 13):
        loads(k).wait()
    for part in range(2):
        cos_t = inner_v[2 * part]
        sin_t = inner_v[2 * part + 1]
        wmat[part, 0:ROWS, 0:ROWS] = cos_t
        wmat[part, ROWS:, ROWS:] = cos_t
        wmat[part, ROWS:, 0:ROWS] = sin_t
        wmat[part, 0:ROWS, ROWS:] = -sin_t

    def thrice(value, dims):
        high, low = split(value)
        return dot(high, wmat[0], dims) + dot(low, wmat[0], dims) + dot(high, wmat[1], dims)

    def stacked(value):
        high, low = split(value)
        return jnp.concatenate([high, low, high], axis=0)

    tr, ti = twist_c[0], twist_c[1]

    def forward(pair):
        z = dot(first_c[...], stacked(jnp.concatenate(pair, axis=1)))
        blocks = []
        for low in range(2):
            cols = slice(ROWS * low, ROWS * low + ROWS)
            zr, zi = z[:RES, cols], z[RES:, cols]
            blocks.append(jnp.concatenate([zr * tr - zi * ti, zr * ti + zi * tr], axis=1))
        return thrice(jnp.concatenate(blocks, axis=0), NN)

    def inverse(x, k):
        gathered(h_send.at[k], h_recv.at[k], h_s.at[k], h_r.at[k], 4 + k)
        wide[...] = h_recv[k].astype(F32)
        blocks = []
        for low in range(2):
            for j in range(2):
                at = low * RES + j * SEQ
                xr, xi = x[at : at + SEQ, :ROWS], x[at : at + SEQ, ROWS:]
                hr = wide[:, j * 2 + low, :]
                hi = wide[:, (2 + j) * 2 + low, :]
                blocks.append(jnp.concatenate([xr * hr - xi * hi, xr * hi + xi * hr], axis=1))
        v = thrice(jnp.concatenate(blocks, axis=0), NT)
        real, imag = [], []
        for low in range(2):
            vr, vi = v[RES * low : RES * low + RES, :ROWS], v[RES * low : RES * low + RES, ROWS:]
            real.append(vr * tr + vi * ti)
            imag.append(vi * tr - vr * ti)
        rhs = jnp.concatenate([jnp.concatenate(real, axis=1), jnp.concatenate(imag, axis=1)], axis=0)
        y = dot(last_c[...], stacked(rhs))
        return [y[:, :ROWS], y[:, ROWS:]]

    at_row = lax.broadcasted_iota(jnp.int32, (SEQ, ROWS), 0)
    at_col = lax.broadcasted_iota(jnp.int32, (SEQ, ROWS), 1)

    def delayed(x, by):
        turned = pltpu.roll(x, by, 1)
        fix = jnp.where(at_row == 0, 0.0, pltpu.roll(turned, 1, 0))
        return jnp.where(at_col < by, fix, turned)

    def filtered(b, i):
        x = wide[:, b * 4 + i, :]
        col = 64 * i + me
        return taps_s[b, 0, col] * x + taps_s[b, 1, col] * delayed(x, 1) + taps_s[b, 2, col] * delayed(x, 2)

    gathered(f_send, f_recv, f_s, f_r, 2)
    wide[...] = f_recv[...].astype(F32)
    values = [filtered(0, i) for i in range(4)]
    gates = [filtered(1, i) for i in range(4)]
    spectra = [forward(values[2 * g : 2 * g + 2]) for g in range(2)]
    carried = []
    for g in range(2):
        ys = inverse(spectra[g], g)
        for low in range(2):
            i = 2 * g + low
            carried.append(gates[i] * (ys[low] + bias_s[0, 64 * i + me] * values[i]))
        spectra[g] = forward(carried[2 * g : 2 * g + 2])

    edge.wait()
    x = f2_v[...].astype(F32)
    edge_rows = jnp.where(me > 0, halo[...].astype(F32), 0.0)
    at = lax.broadcasted_iota(jnp.int32, (ROWS, CH), 0)
    one = jnp.where(at == 0, edge_rows[15:16], pltpu.roll(x, 1, 0))
    two = jnp.where(at == 0, edge_rows[14:15], jnp.where(at == 1, edge_rows[15:16], pltpu.roll(x, 2, 0)))
    gate_v[...] = taps_v[2, 0:1, :] * x + taps_v[2, 1:2, :] * one + taps_v[2, 2:3, :] * two

    for g in range(2):
        ys = inverse(spectra[g], 2 + g)
        for low in range(2):
            i = 2 * g + low
            wide[:, low, :] = ys[low] + bias_s[1, 64 * i + me] * carried[i]
        u_send[g] = wide[:, 0:2, :].astype(BF)
        spread(u_send.at[g], u_recv.at[g], u_s.at[g], u_r.at[g], 8 + g)

    for g in range(2):
        gathered(u_send.at[g], u_recv.at[g], u_s.at[g], u_r.at[g], 8 + g)
        wide[:, 0:2, :] = u_recv[g].astype(F32)
        turned = jnp.concatenate([wide[:, low, :] for low in range(2)], axis=0).T
        lanes = slice(128 * g, 128 * g + 128)
        g_send[g] = (gate_v[:, lanes] * turned).astype(BF).reshape(TP, OUT_ROWS, 128)
        for t in range(1, TP):
            x_copy(g_send.at[g, (mx + t) % TP], g_recv.at[g, mx], g_s.at[g], g_r.at[g], t).start()
        own_copy(g_send.at[g, mx], g_recv.at[g, mx], 10 + g).start()
    own_copy(w_out, wg.at[mx], 1).wait()
    pltpu.make_async_copy(wg.at[pl.ds(0, 3)], wg.at[pl.ds(0, 3)], wo_r).wait()
    parts = []
    for g in range(2):
        own_copy(g_send.at[g, mx], g_recv.at[g, mx], 10 + g).wait()
        pltpu.make_async_copy(g_recv.at[g, pl.ds(0, 3)], g_recv.at[g, pl.ds(0, 3)], g_r.at[g]).wait()
        line = jnp.concatenate([g_recv[g, t] for t in range(TP)], axis=1)
        parts.append(dot(line, wg[:, g].reshape(512, 1024)))
    out[...] = (parts[0] + parts[1]).astype(BF)

    pltpu.make_async_copy(tg.at[pl.ds(0, 3)], tg.at[pl.ds(0, 3)], tok_s).wait()
    pltpu.make_async_copy(wg.at[pl.ds(0, 3)], wg.at[pl.ds(0, 3)], wo_s).wait()
    for k in range(4):
        sent(h_send.at[k], h_s.at[k])
    sent(f_send, f_s)
    for g in range(2):
        sent(u_send.at[g], u_s.at[g])
        pltpu.make_async_copy(g_send.at[g, pl.ds(0, 3)], g_send.at[g, pl.ds(0, 3)], g_s.at[g]).wait()


def local(tokens, w_in, short_taps, skip_bias, filter_spectra, w_out):
    inner_table, first_table, last_table, twist, pick = tables()
    vmem = pl.BlockSpec(memory_space=pltpu.VMEM)
    hbm = pl.BlockSpec(memory_space=pltpu.HBM)
    dma = pltpu.SemaphoreType.DMA
    return pl.pallas_call(
        body,
        out_shape=jax.ShapeDtypeStruct((OUT_ROWS, 1024), BF),
        in_specs=[hbm] * 11,
        out_specs=vmem,
        scratch_shapes=[
            pltpu.SMEM((3, 3, CH), F32),
            pltpu.SMEM((2, CH), F32),
            pltpu.VMEM((3, 3, CH), F32),
            pltpu.VMEM((2 * RES, 3 * SEQ), BF),
            pltpu.VMEM((SEQ, 6 * RES), BF),
            pltpu.VMEM((2, RES, ROWS), F32),
            pltpu.VMEM((512, 512), BF),
            pltpu.VMEM((2, 2, 2, ROWS, CH), F32),
            pltpu.VMEM((3, 1024, CH), BF),
            pltpu.VMEM((4, ROWS, ROWS), BF),
            pltpu.VMEM((2, 2 * ROWS, 2 * ROWS), BF),
            pltpu.VMEM((TP, OUT_ROWS, 1024), BF),
            pltpu.VMEM((TP, 2, 128, 1024), BF),
            pltpu.VMEM((4, SEQ, 8, ROWS), BF),
            pltpu.VMEM((4, SEQ, 8, ROWS), BF),
            pltpu.VMEM((SEQ, 8, ROWS), BF),
            pltpu.VMEM((SEQ, 8, ROWS), BF),
            pltpu.VMEM((2, SEQ, 2, ROWS), BF),
            pltpu.VMEM((2, SEQ, 2, ROWS), BF),
            pltpu.VMEM((SEQ, 8, ROWS), F32),
            pltpu.VMEM((ROWS, CH), BF),
            pltpu.VMEM((16, CH), BF),
            pltpu.VMEM((ROWS, CH), F32),
            pltpu.VMEM((2, TP, OUT_ROWS, 128), BF),
            pltpu.VMEM((2, TP, OUT_ROWS, 128), BF),
            dma((13,)),
            dma((12,)),
            dma, dma, dma, dma,
            dma((4,)),
            dma((4,)),
            dma, dma, dma, dma, dma((2,)), dma((2,)), dma((2,)), dma((2,)),
        ],
        compiler_params=pltpu.CompilerParams(
            collective_id=0, has_side_effects=True, vmem_limit_bytes=40 * 1024 * 1024
        ),
    )(
        *[pltpu.with_memory_space_constraint(item, pltpu.HBM) for item in (
        tokens, w_in, short_taps, skip_bias, filter_spectra, w_out.reshape(2, 128, 1024),
        jnp.asarray(inner_table), jnp.asarray(first_table), jnp.asarray(last_table),
        jnp.asarray(twist), jnp.asarray(pick),
            )]
    )


def solution(mesh):
    in_specs = (
        P(("seq", "tp"), None),
        P(None, None, "tp"),
        P(None, None, "tp"),
        P(None, "tp"),
        P(None, None, "seq", None, "tp"),
        P("tp", None),
    )
    out_specs = P(("seq", "tp"), None)
    return jax.shard_map(local, mesh=mesh, in_specs=in_specs, out_specs=out_specs, check_vma=False)
```

```python
import math

import jax
import jax.numpy as jnp
import ml_dtypes
import numpy as np
from jax import lax
from jax.experimental import pallas as pl
from jax.experimental.pallas import tpu as pltpu
from jax.sharding import PartitionSpec as P

MESH = pl.DeviceIdType.MESH
BF = jnp.bfloat16
F32 = jnp.float32
SEQ, TP = 64, 4
ROWS, CH, OUT_ROWS = 384, 256, 96
RES = 128
NT = (((1,), (1,)), ((), ()))
NN = (((1,), (0,)), ((), ()))


def halves(table):
    high = table.astype(ml_dtypes.bfloat16)
    low = (table - high.astype(np.float64)).astype(ml_dtypes.bfloat16)
    return high, low


def tables():
    total = RES * ROWS
    line = np.arange(ROWS)
    inner = 2.0 * np.pi / ROWS * (np.outer(line, line) % ROWS)
    cos_hi, cos_lo = halves(np.cos(inner))
    sin_hi, sin_lo = halves(np.sin(inner))
    inner_table = np.stack([cos_hi, sin_hi, cos_lo, sin_lo])
    order = np.concatenate([2 * np.arange(SEQ), 2 * np.arange(SEQ) + 1])
    outer = 2.0 * np.pi / RES * (np.outer(order, np.arange(SEQ)) % RES)
    first = np.concatenate([np.cos(outer), -np.sin(outer)], axis=0)
    first_hi, first_lo = halves(first)
    first_table = np.concatenate([first_hi, first_hi, first_lo], axis=1)
    last = np.concatenate([np.cos(outer.T), -np.sin(outer.T)], axis=1) / total
    last_hi, last_lo = halves(last)
    last_table = np.concatenate([last_hi, last_hi, last_lo], axis=1)
    angle = -2.0 * np.pi / total * np.outer(order, line)
    twist = np.stack([np.cos(angle), np.sin(angle)]).astype(np.float32)
    pick = np.zeros((512, 512), ml_dtypes.bfloat16)
    for dest in range(SEQ):
        for slot in range(4):
            for low in range(2):
                pick[dest * 8 + slot * 2 + low, slot * 128 + low * 64 + dest] = 1
    return inner_table, first_table, last_table, twist, pick


def split(value):
    high = value.astype(BF)
    low = (value - high.astype(F32)).astype(BF)
    return high, low


def dot(a, b, dims=NN):
    return lax.dot_general(a, b, dims, preferred_element_type=F32)


def body(
    tok, w_in, taps_h, bias_h, spec, w_out, inner_h, first_h, last_h, twist_h, pick_h,
    out,
    taps_s, bias_s, taps_v, first_c, last_c, twist_c, pick_c, spec_v, w_in_v, inner_v, wmat, tg, wg, h_send, h_recv, f_send, f_recv, u_send, u_recv,
    wide, f2_v, halo, gate_v, g_send, g_recv,
    load_sem, own_sem, tok_s, tok_r, wo_s, wo_r, h_s, h_r, f_s, f_r, halo_s, halo_r, u_s, u_r, g_s, g_r,
):
    me = lax.axis_index("seq")
    mx = lax.axis_index("tp")

    def peer(i):
        to = me + i
        return jnp.where(to >= SEQ, to - SEQ, to)

    barrier = pltpu.get_barrier_semaphore()

    def greet(i, carry):
        pl.semaphore_signal(barrier, inc=1, device_id={"seq": peer(i)}, device_id_type=MESH)
        return carry

    lax.fori_loop(1, SEQ, greet, 0, unroll=7)
    for t in range(1, TP):
        pl.semaphore_signal(barrier, inc=1, device_id={"tp": (mx + t) % TP}, device_id_type=MESH)

    def half(ref, o, g):
        return ref.at[o, :, :, :, pl.ds(128 * g, 128)]

    def loads(k):
        pairs = (
            (half(spec, 0, 0), half(spec_v, 0, 0)), (pick_h, pick_c), (half(spec, 0, 1), half(spec_v, 0, 1)),
            (w_in, w_in_v), (half(spec, 1, 0), half(spec_v, 1, 0)), (half(spec, 1, 1), half(spec_v, 1, 1)),
            (inner_h, inner_v), (first_h, first_c), (twist_h, twist_c), (last_h, last_c),
            (taps_h, taps_v), (taps_h, taps_s), (bias_h, bias_s),
        )
        return pltpu.make_async_copy(pairs[k][0], pairs[k][1], load_sem.at[k])

    for k in range(13):
        loads(k).start()

    def x_copy(src, dst, ssem, rsem, t):
        return pltpu.make_async_remote_copy(
            src, dst, ssem, rsem, device_id={"tp": (mx + t) % TP}, device_id_type=MESH
        )

    def own_copy(src, dst, k):
        return pltpu.make_async_copy(src, dst, own_sem.at[k])

    def all_wait(src_slice, dst_slice, ssem, rsem):
        pltpu.make_async_copy(src_slice, src_slice, ssem).wait()
        pltpu.make_async_copy(dst_slice, dst_slice, rsem).wait()

    def spread(send, recv, ssem, rsem, k):
        def one(i, carry):
            to = peer(i)
            pltpu.make_async_remote_copy(
                send.at[to], recv.at[me], ssem, rsem, device_id={"seq": to}, device_id_type=MESH
            ).start()
            return carry

        lax.fori_loop(1, SEQ, one, 0, unroll=7)
        own_copy(send.at[me], recv.at[me], k).start()

    def gathered(send, recv, ssem, rsem, k):
        own_copy(send.at[me], recv.at[me], k).wait()
        pltpu.make_async_copy(recv.at[pl.ds(0, SEQ - 1)], recv.at[pl.ds(0, SEQ - 1)], rsem).wait()

    def sent(send, ssem):
        pltpu.make_async_copy(send.at[pl.ds(0, SEQ - 1)], send.at[pl.ds(0, SEQ - 1)], ssem).wait()

    def turn_filter(o, g):
        k = 2 * o + g
        lanes = slice(128 * g, 128 * g + 128)
        line = jnp.concatenate(
            [spec_v[o, ri, j, :, lanes].astype(BF) for ri in range(2) for j in range(2)], axis=1
        )
        turned = dot(pick_c[...], line, NT)
        h_send[k] = turned.reshape(SEQ, 8, ROWS).astype(BF)

    def ship_filter(k):
        spread(h_send.at[k], h_recv.at[k], h_s.at[k], h_r.at[k], 4 + k)

    loads(0).wait()
    loads(1).wait()
    turn_filter(0, 0)
    pl.semaphore_wait(barrier, SEQ - 1 + TP - 1)
    for t in range(1, TP):
        x_copy(tok, tg.at[mx], tok_s, tok_r, t).start()
    own_copy(tok, tg.at[mx], 0).start()
    ship_filter(0)
    loads(2).wait()
    turn_filter(0, 1)
    ship_filter(1)

    for t in range(1, TP):
        x_copy(w_out, wg.at[mx], wo_s, wo_r, t).start()
    own_copy(w_out, wg.at[mx], 1).start()

    loads(3).wait()
    own_copy(tok, tg.at[mx], 0).wait()
    pltpu.make_async_copy(tg.at[pl.ds(0, 3)], tg.at[pl.ds(0, 3)], tok_r).wait()
    rows = tg[...].reshape(ROWS, 1024)
    lines = [dot(rows, w_in_v[b]).astype(BF) for b in range(3)]
    turned = dot(pick_c[...], jnp.concatenate(lines[:2], axis=1), NT)
    f_send[...] = turned.reshape(SEQ, 8, ROWS).astype(BF)
    spread(f_send, f_recv, f_s, f_r, 2)
    f2_v[...] = lines[2]
    after = (me + 1) % SEQ
    edge = pltpu.make_async_remote_copy(
        f2_v.at[pl.ds(ROWS - 16, 16)], halo, halo_s, halo_r, device_id={"seq": after}, device_id_type=MESH
    )
    edge.start()

    for g in range(2):
        loads(4 + g).wait()
        turn_filter(1, g)
        ship_filter(2 + g)

    for k in range(6, 13):
        loads(k).wait()
    for part in range(2):
        cos_t = inner_v[2 * part]
        sin_t = inner_v[2 * part + 1]
        wmat[part, 0:ROWS, 0:ROWS] = cos_t
        wmat[part, ROWS:, ROWS:] = cos_t
        wmat[part, ROWS:, 0:ROWS] = sin_t
        wmat[part, 0:ROWS, ROWS:] = -sin_t

    def thrice(value, dims):
        high, low = split(value)
        return dot(high, wmat[0], dims) + dot(low, wmat[0], dims) + dot(high, wmat[1], dims)

    def stacked(value):
        high, low = split(value)
        return jnp.concatenate([high, low, high], axis=0)

    tr, ti = twist_c[0], twist_c[1]

    def forward(pair):
        z = dot(first_c[...], stacked(jnp.concatenate(pair, axis=1)))
        blocks = []
        for low in range(2):
            cols = slice(ROWS * low, ROWS * low + ROWS)
            zr, zi = z[:RES, cols], z[RES:, cols]
            blocks.append(jnp.concatenate([zr * tr - zi * ti, zr * ti + zi * tr], axis=1))
        return thrice(jnp.concatenate(blocks, axis=0), NN)

    def inverse(x, k):
        gathered(h_send.at[k], h_recv.at[k], h_s.at[k], h_r.at[k], 4 + k)
        wide[...] = h_recv[k].astype(F32)
        blocks = []
        for low in range(2):
            for j in range(2):
                at = low * RES + j * SEQ
                xr, xi = x[at : at + SEQ, :ROWS], x[at : at + SEQ, ROWS:]
                hr = wide[:, j * 2 + low, :]
                hi = wide[:, (2 + j) * 2 + low, :]
                blocks.append(jnp.concatenate([xr * hr - xi * hi, xr * hi + xi * hr], axis=1))
        lines_in = jnp.concatenate(blocks, axis=0)
        v = thrice(lines_in, NT) if k < 2 else dot(lines_in.astype(BF), wmat[0], NT)
        real, imag = [], []
        for low in range(2):
            vr, vi = v[RES * low : RES * low + RES, :ROWS], v[RES * low : RES * low + RES, ROWS:]
            real.append(vr * tr + vi * ti)
            imag.append(vi * tr - vr * ti)
        rhs = jnp.concatenate([jnp.concatenate(real, axis=1), jnp.concatenate(imag, axis=1)], axis=0)
        y = dot(last_c[...], stacked(rhs)) if k < 2 else dot(last_c[:, : 2 * RES], rhs.astype(BF))
        return [y[:, :ROWS], y[:, ROWS:]]

    at_row = lax.broadcasted_iota(jnp.int32, (SEQ, ROWS), 0)
    at_col = lax.broadcasted_iota(jnp.int32, (SEQ, ROWS), 1)

    def delayed(x, by):
        turned = pltpu.roll(x, by, 1)
        fix = jnp.where(at_row == 0, 0.0, pltpu.roll(turned, 1, 0))
        return jnp.where(at_col < by, fix, turned)

    def filtered(b, i):
        x = wide[:, b * 4 + i, :]
        col = 64 * i + me
        return taps_s[b, 0, col] * x + taps_s[b, 1, col] * delayed(x, 1) + taps_s[b, 2, col] * delayed(x, 2)

    gathered(f_send, f_recv, f_s, f_r, 2)
    wide[...] = f_recv[...].astype(F32)
    values = [filtered(0, i) for i in range(4)]
    gates = [filtered(1, i) for i in range(4)]
    spectra = [forward(values[2 * g : 2 * g + 2]) for g in range(2)]
    carried = []
    for g in range(2):
        ys = inverse(spectra[g], g)
        for low in range(2):
            i = 2 * g + low
            carried.append(gates[i] * (ys[low] + bias_s[0, 64 * i + me] * values[i]))
        spectra[g] = forward(carried[2 * g : 2 * g + 2])

    edge.wait()
    x = f2_v[...].astype(F32)
    edge_rows = jnp.where(me > 0, halo[...].astype(F32), 0.0)
    at = lax.broadcasted_iota(jnp.int32, (ROWS, CH), 0)
    one = jnp.where(at == 0, edge_rows[15:16], pltpu.roll(x, 1, 0))
    two = jnp.where(at == 0, edge_rows[14:15], jnp.where(at == 1, edge_rows[15:16], pltpu.roll(x, 2, 0)))
    gate_v[...] = taps_v[2, 0:1, :] * x + taps_v[2, 1:2, :] * one + taps_v[2, 2:3, :] * two

    for g in range(2):
        ys = inverse(spectra[g], 2 + g)
        for low in range(2):
            i = 2 * g + low
            wide[:, low, :] = ys[low] + bias_s[1, 64 * i + me] * carried[i]
        u_send[g] = wide[:, 0:2, :].astype(BF)
        spread(u_send.at[g], u_recv.at[g], u_s.at[g], u_r.at[g], 8 + g)

    for g in range(2):
        gathered(u_send.at[g], u_recv.at[g], u_s.at[g], u_r.at[g], 8 + g)
        wide[:, 0:2, :] = u_recv[g].astype(F32)
        turned = jnp.concatenate([wide[:, low, :] for low in range(2)], axis=0).T
        lanes = slice(128 * g, 128 * g + 128)
        g_send[g] = (gate_v[:, lanes] * turned).astype(BF).reshape(TP, OUT_ROWS, 128)
        for t in (2, 1, 3):
            x_copy(g_send.at[g, (mx + t) % TP], g_recv.at[g, mx], g_s.at[g], g_r.at[g], t).start()
        own_copy(g_send.at[g, mx], g_recv.at[g, mx], 10 + g).start()
    own_copy(w_out, wg.at[mx], 1).wait()
    pltpu.make_async_copy(wg.at[pl.ds(0, 3)], wg.at[pl.ds(0, 3)], wo_r).wait()
    parts = []
    for g in range(2):
        own_copy(g_send.at[g, mx], g_recv.at[g, mx], 10 + g).wait()
        pltpu.make_async_copy(g_recv.at[g, pl.ds(0, 3)], g_recv.at[g, pl.ds(0, 3)], g_r.at[g]).wait()
        line = jnp.concatenate([g_recv[g, t] for t in range(TP)], axis=1)
        parts.append(dot(line, wg[:, g].reshape(512, 1024)))
    out[...] = (parts[0] + parts[1]).astype(BF)

    pltpu.make_async_copy(tg.at[pl.ds(0, 3)], tg.at[pl.ds(0, 3)], tok_s).wait()
    pltpu.make_async_copy(wg.at[pl.ds(0, 3)], wg.at[pl.ds(0, 3)], wo_s).wait()
    for k in range(4):
        sent(h_send.at[k], h_s.at[k])
    sent(f_send, f_s)
    for g in range(2):
        sent(u_send.at[g], u_s.at[g])
        pltpu.make_async_copy(g_send.at[g, pl.ds(0, 3)], g_send.at[g, pl.ds(0, 3)], g_s.at[g]).wait()


def local(tokens, w_in, short_taps, skip_bias, filter_spectra, w_out):
    inner_table, first_table, last_table, twist, pick = tables()
    vmem = pl.BlockSpec(memory_space=pltpu.VMEM)
    hbm = pl.BlockSpec(memory_space=pltpu.HBM)
    dma = pltpu.SemaphoreType.DMA
    return pl.pallas_call(
        body,
        out_shape=jax.ShapeDtypeStruct((OUT_ROWS, 1024), BF),
        in_specs=[hbm] * 11,
        out_specs=vmem,
        scratch_shapes=[
            pltpu.SMEM((3, 3, CH), F32),
            pltpu.SMEM((2, CH), F32),
            pltpu.VMEM((3, 3, CH), F32),
            pltpu.VMEM((2 * RES, 3 * SEQ), BF),
            pltpu.VMEM((SEQ, 6 * RES), BF),
            pltpu.VMEM((2, RES, ROWS), F32),
            pltpu.VMEM((512, 512), BF),
            pltpu.VMEM((2, 2, 2, ROWS, CH), F32),
            pltpu.VMEM((3, 1024, CH), BF),
            pltpu.VMEM((4, ROWS, ROWS), BF),
            pltpu.VMEM((2, 2 * ROWS, 2 * ROWS), BF),
            pltpu.VMEM((TP, OUT_ROWS, 1024), BF),
            pltpu.VMEM((TP, 2, 128, 1024), BF),
            pltpu.VMEM((4, SEQ, 8, ROWS), BF),
            pltpu.VMEM((4, SEQ, 8, ROWS), BF),
            pltpu.VMEM((SEQ, 8, ROWS), BF),
            pltpu.VMEM((SEQ, 8, ROWS), BF),
            pltpu.VMEM((2, SEQ, 2, ROWS), BF),
            pltpu.VMEM((2, SEQ, 2, ROWS), BF),
            pltpu.VMEM((SEQ, 8, ROWS), F32),
            pltpu.VMEM((ROWS, CH), BF),
            pltpu.VMEM((16, CH), BF),
            pltpu.VMEM((ROWS, CH), F32),
            pltpu.VMEM((2, TP, OUT_ROWS, 128), BF),
            pltpu.VMEM((2, TP, OUT_ROWS, 128), BF),
            dma((13,)),
            dma((12,)),
            dma, dma, dma, dma,
            dma((4,)),
            dma((4,)),
            dma, dma, dma, dma, dma((2,)), dma((2,)), dma((2,)), dma((2,)),
        ],
        compiler_params=pltpu.CompilerParams(
            collective_id=0, has_side_effects=True, vmem_limit_bytes=40 * 1024 * 1024
        ),
    )(
        *[pltpu.with_memory_space_constraint(item, pltpu.HBM) for item in (
        tokens, w_in, short_taps, skip_bias, filter_spectra, w_out.reshape(2, 128, 1024),
        jnp.asarray(inner_table), jnp.asarray(first_table), jnp.asarray(last_table),
        jnp.asarray(twist), jnp.asarray(pick),
            )]
    )


def solution(mesh):
    in_specs = (
        P(("seq", "tp"), None),
        P(None, None, "tp"),
        P(None, None, "tp"),
        P(None, "tp"),
        P(None, None, "seq", None, "tp"),
        P("tp", None),
    )
    out_specs = P(("seq", "tp"), None)
    return jax.shard_map(local, mesh=mesh, in_specs=in_specs, out_specs=out_specs, check_vma=False)
```

```python
import math

import jax
import jax.numpy as jnp
import ml_dtypes
import numpy as np
from jax import lax
from jax.experimental import pallas as pl
from jax.experimental.pallas import tpu as pltpu
from jax.sharding import PartitionSpec as P

MESH = pl.DeviceIdType.MESH
BF = jnp.bfloat16
F32 = jnp.float32
SEQ, TP = 64, 4
ROWS, CH, OUT_ROWS = 384, 256, 96
RES = 128
NT = (((1,), (1,)), ((), ()))
NN = (((1,), (0,)), ((), ()))


def halves(table):
    high = table.astype(ml_dtypes.bfloat16)
    low = (table - high.astype(np.float64)).astype(ml_dtypes.bfloat16)
    return high, low


def tables():
    total = RES * ROWS
    line = np.arange(ROWS)
    inner = 2.0 * np.pi / ROWS * (np.outer(line, line) % ROWS)
    cos_hi, cos_lo = halves(np.cos(inner))
    sin_hi, sin_lo = halves(np.sin(inner))
    inner_table = np.stack([cos_hi, sin_hi, cos_lo, sin_lo])
    order = np.concatenate([2 * np.arange(SEQ), 2 * np.arange(SEQ) + 1])
    outer = 2.0 * np.pi / RES * (np.outer(order, np.arange(SEQ)) % RES)
    first = np.concatenate([np.cos(outer), -np.sin(outer)], axis=0)
    first_hi, first_lo = halves(first)
    first_table = np.concatenate([first_hi, first_hi, first_lo], axis=1)
    last = np.concatenate([np.cos(outer.T), -np.sin(outer.T)], axis=1) / total
    last_hi, last_lo = halves(last)
    last_table = np.concatenate([last_hi, last_hi, last_lo], axis=1)
    angle = -2.0 * np.pi / total * np.outer(order, line)
    twist = np.stack([np.cos(angle), np.sin(angle)]).astype(np.float32)
    pick = np.zeros((512, 512), ml_dtypes.bfloat16)
    for dest in range(SEQ):
        for slot in range(4):
            for low in range(2):
                pick[dest * 8 + slot * 2 + low, slot * 128 + low * 64 + dest] = 1
    return inner_table, first_table, last_table, twist, pick


def split(value):
    high = value.astype(BF)
    low = (value - high.astype(F32)).astype(BF)
    return high, low


def dot(a, b, dims=NN):
    return lax.dot_general(a, b, dims, preferred_element_type=F32)


def body(
    tok, w_in, taps_h, bias_h, spec, w_out, inner_h, first_h, last_h, twist_h, pick_h,
    out,
    taps_s, bias_s, taps_v, first_c, last_c, twist_c, pick_c, spec_v, w_in_v, inner_v, wmat, tg, wg, h_send, h_recv, f_send, f_recv, u_send, u_recv,
    wide, f2_v, halo, gate_v, g_send, g_recv,
    load_sem, own_sem, tok_s, tok_r, wo_s, wo_r, h_s, h_r, f_s, f_r, halo_s, halo_r, u_s, u_r, g_s, g_r,
):
    me = lax.axis_index("seq")
    mx = lax.axis_index("tp")

    def peer(i):
        to = me + i
        return jnp.where(to >= SEQ, to - SEQ, to)

    barrier = pltpu.get_barrier_semaphore()

    def greet(i, carry):
        pl.semaphore_signal(barrier, inc=1, device_id={"seq": peer(i)}, device_id_type=MESH)
        return carry

    lax.fori_loop(1, SEQ, greet, 0, unroll=7)
    for t in range(1, TP):
        pl.semaphore_signal(barrier, inc=1, device_id={"tp": (mx + t) % TP}, device_id_type=MESH)

    def half(ref, o, g):
        return ref.at[o, :, :, :, pl.ds(128 * g, 128)]

    def loads(k):
        pairs = (
            (half(spec, 0, 0), half(spec_v, 0, 0)), (pick_h, pick_c), (half(spec, 0, 1), half(spec_v, 0, 1)),
            (w_in, w_in_v), (half(spec, 1, 0), half(spec_v, 1, 0)), (half(spec, 1, 1), half(spec_v, 1, 1)),
            (inner_h, inner_v), (first_h, first_c), (twist_h, twist_c), (last_h, last_c),
            (taps_h, taps_v), (taps_h, taps_s), (bias_h, bias_s),
        )
        return pltpu.make_async_copy(pairs[k][0], pairs[k][1], load_sem.at[k])

    for k in range(13):
        loads(k).start()

    def x_copy(src, dst, ssem, rsem, t):
        return pltpu.make_async_remote_copy(
            src, dst, ssem, rsem, device_id={"tp": (mx + t) % TP}, device_id_type=MESH
        )

    def own_copy(src, dst, k):
        return pltpu.make_async_copy(src, dst, own_sem.at[k])

    def all_wait(src_slice, dst_slice, ssem, rsem):
        pltpu.make_async_copy(src_slice, src_slice, ssem).wait()
        pltpu.make_async_copy(dst_slice, dst_slice, rsem).wait()

    def spread(send, recv, ssem, rsem, k):
        def one(i, carry):
            to = peer(i)
            pltpu.make_async_remote_copy(
                send.at[to], recv.at[me], ssem, rsem, device_id={"seq": to}, device_id_type=MESH
            ).start()
            return carry

        lax.fori_loop(1, SEQ, one, 0, unroll=63 if k >= 8 else 7)
        own_copy(send.at[me], recv.at[me], k).start()

    def gathered(send, recv, ssem, rsem, k):
        own_copy(send.at[me], recv.at[me], k).wait()
        pltpu.make_async_copy(recv.at[pl.ds(0, SEQ - 1)], recv.at[pl.ds(0, SEQ - 1)], rsem).wait()

    def sent(send, ssem):
        pltpu.make_async_copy(send.at[pl.ds(0, SEQ - 1)], send.at[pl.ds(0, SEQ - 1)], ssem).wait()

    def turn_filter(o, g):
        k = 2 * o + g
        lanes = slice(128 * g, 128 * g + 128)
        line = jnp.concatenate(
            [spec_v[o, ri, j, :, lanes].astype(BF) for ri in range(2) for j in range(2)], axis=1
        )
        turned = dot(pick_c[...], line, NT)
        h_send[k] = turned.reshape(SEQ, 8, ROWS).astype(BF)

    def ship_filter(k):
        spread(h_send.at[k], h_recv.at[k], h_s.at[k], h_r.at[k], 4 + k)

    loads(0).wait()
    loads(1).wait()
    turn_filter(0, 0)
    pl.semaphore_wait(barrier, SEQ - 1 + TP - 1)
    for t in range(1, TP):
        x_copy(tok, tg.at[mx], tok_s, tok_r, t).start()
    own_copy(tok, tg.at[mx], 0).start()
    ship_filter(0)
    loads(2).wait()
    turn_filter(0, 1)
    ship_filter(1)

    for t in range(1, TP):
        x_copy(w_out, wg.at[mx], wo_s, wo_r, t).start()
    own_copy(w_out, wg.at[mx], 1).start()

    loads(3).wait()
    own_copy(tok, tg.at[mx], 0).wait()
    pltpu.make_async_copy(tg.at[pl.ds(0, 3)], tg.at[pl.ds(0, 3)], tok_r).wait()
    rows = tg[...].reshape(ROWS, 1024)
    lines = [dot(rows, w_in_v[b]).astype(BF) for b in range(3)]
    turned = dot(pick_c[...], jnp.concatenate(lines[:2], axis=1), NT)
    f_send[...] = turned.reshape(SEQ, 8, ROWS).astype(BF)
    spread(f_send, f_recv, f_s, f_r, 2)
    f2_v[...] = lines[2]
    after = (me + 1) % SEQ
    edge = pltpu.make_async_remote_copy(
        f2_v.at[pl.ds(ROWS - 16, 16)], halo, halo_s, halo_r, device_id={"seq": after}, device_id_type=MESH
    )
    edge.start()

    for g in range(2):
        loads(4 + g).wait()
        turn_filter(1, g)
        ship_filter(2 + g)

    for k in range(6, 13):
        loads(k).wait()
    for part in range(2):
        cos_t = inner_v[2 * part]
        sin_t = inner_v[2 * part + 1]
        wmat[part, 0:ROWS, 0:ROWS] = cos_t
        wmat[part, ROWS:, ROWS:] = cos_t
        wmat[part, ROWS:, 0:ROWS] = sin_t
        wmat[part, 0:ROWS, ROWS:] = -sin_t

    def thrice(value, dims):
        high, low = split(value)
        return dot(high, wmat[0], dims) + dot(low, wmat[0], dims) + dot(high, wmat[1], dims)

    def stacked(value):
        high, low = split(value)
        return jnp.concatenate([high, low, high], axis=0)

    tr, ti = twist_c[0], twist_c[1]

    def forward(pair):
        z = dot(first_c[...], stacked(jnp.concatenate(pair, axis=1)))
        blocks = []
        for low in range(2):
            cols = slice(ROWS * low, ROWS * low + ROWS)
            zr, zi = z[:RES, cols], z[RES:, cols]
            blocks.append(jnp.concatenate([zr * tr - zi * ti, zr * ti + zi * tr], axis=1))
        return thrice(jnp.concatenate(blocks, axis=0), NN)

    def inverse(x, k):
        gathered(h_send.at[k], h_recv.at[k], h_s.at[k], h_r.at[k], 4 + k)
        wide[...] = h_recv[k].astype(F32)
        blocks = []
        for low in range(2):
            for j in range(2):
                at = low * RES + j * SEQ
                xr, xi = x[at : at + SEQ, :ROWS], x[at : at + SEQ, ROWS:]
                hr = wide[:, j * 2 + low, :]
                hi = wide[:, (2 + j) * 2 + low, :]
                blocks.append(jnp.concatenate([xr * hr - xi * hi, xr * hi + xi * hr], axis=1))
        lines_in = jnp.concatenate(blocks, axis=0)
        v = thrice(lines_in, NT) if k < 2 else dot(lines_in.astype(BF), wmat[0], NT)
        real, imag = [], []
        for low in range(2):
            vr, vi = v[RES * low : RES * low + RES, :ROWS], v[RES * low : RES * low + RES, ROWS:]
            real.append(vr * tr + vi * ti)
            imag.append(vi * tr - vr * ti)
        rhs = jnp.concatenate([jnp.concatenate(real, axis=1), jnp.concatenate(imag, axis=1)], axis=0)
        y = dot(last_c[...], stacked(rhs)) if k < 2 else dot(last_c[:, : 2 * RES], rhs.astype(BF))
        return [y[:, :ROWS], y[:, ROWS:]]

    at_row = lax.broadcasted_iota(jnp.int32, (SEQ, ROWS), 0)
    at_col = lax.broadcasted_iota(jnp.int32, (SEQ, ROWS), 1)

    def delayed(x, by):
        turned = pltpu.roll(x, by, 1)
        fix = jnp.where(at_row == 0, 0.0, pltpu.roll(turned, 1, 0))
        return jnp.where(at_col < by, fix, turned)

    def filtered(b, i):
        x = wide[:, b * 4 + i, :]
        col = 64 * i + me
        return taps_s[b, 0, col] * x + taps_s[b, 1, col] * delayed(x, 1) + taps_s[b, 2, col] * delayed(x, 2)

    gathered(f_send, f_recv, f_s, f_r, 2)
    wide[...] = f_recv[...].astype(F32)
    values = [filtered(0, i) for i in range(4)]
    gates = [filtered(1, i) for i in range(4)]
    spectra = [forward(values[2 * g : 2 * g + 2]) for g in range(2)]
    carried = []
    for g in range(2):
        ys = inverse(spectra[g], g)
        for low in range(2):
            i = 2 * g + low
            carried.append(gates[i] * (ys[low] + bias_s[0, 64 * i + me] * values[i]))
        spectra[g] = forward(carried[2 * g : 2 * g + 2])

    edge.wait()
    x = f2_v[...].astype(F32)
    edge_rows = jnp.where(me > 0, halo[...].astype(F32), 0.0)
    at = lax.broadcasted_iota(jnp.int32, (ROWS, CH), 0)
    one = jnp.where(at == 0, edge_rows[15:16], pltpu.roll(x, 1, 0))
    two = jnp.where(at == 0, edge_rows[14:15], jnp.where(at == 1, edge_rows[15:16], pltpu.roll(x, 2, 0)))
    gate_v[...] = taps_v[2, 0:1, :] * x + taps_v[2, 1:2, :] * one + taps_v[2, 2:3, :] * two

    for g in range(2):
        ys = inverse(spectra[g], 2 + g)
        for low in range(2):
            i = 2 * g + low
            wide[:, low, :] = ys[low] + bias_s[1, 64 * i + me] * carried[i]
        u_send[g] = wide[:, 0:2, :].astype(BF)
        spread(u_send.at[g], u_recv.at[g], u_s.at[g], u_r.at[g], 8 + g)

    for g in range(2):
        gathered(u_send.at[g], u_recv.at[g], u_s.at[g], u_r.at[g], 8 + g)
        wide[:, 0:2, :] = u_recv[g].astype(F32)
        turned = jnp.concatenate([wide[:, low, :] for low in range(2)], axis=0).T
        lanes = slice(128 * g, 128 * g + 128)
        g_send[g] = (gate_v[:, lanes] * turned).astype(BF).reshape(TP, OUT_ROWS, 128)
        for t in (2, 1, 3):
            x_copy(g_send.at[g, (mx + t) % TP], g_recv.at[g, mx], g_s.at[g], g_r.at[g], t).start()
        own_copy(g_send.at[g, mx], g_recv.at[g, mx], 10 + g).start()
    own_copy(w_out, wg.at[mx], 1).wait()
    pltpu.make_async_copy(wg.at[pl.ds(0, 3)], wg.at[pl.ds(0, 3)], wo_r).wait()
    parts = []
    for g in range(2):
        own_copy(g_send.at[g, mx], g_recv.at[g, mx], 10 + g).wait()
        pltpu.make_async_copy(g_recv.at[g, pl.ds(0, 3)], g_recv.at[g, pl.ds(0, 3)], g_r.at[g]).wait()
        line = jnp.concatenate([g_recv[g, t] for t in range(TP)], axis=1)
        parts.append(dot(line, wg[:, g].reshape(512, 1024)))
    out[...] = (parts[0] + parts[1]).astype(BF)

    pltpu.make_async_copy(tg.at[pl.ds(0, 3)], tg.at[pl.ds(0, 3)], tok_s).wait()
    pltpu.make_async_copy(wg.at[pl.ds(0, 3)], wg.at[pl.ds(0, 3)], wo_s).wait()
    for k in range(4):
        sent(h_send.at[k], h_s.at[k])
    sent(f_send, f_s)
    for g in range(2):
        sent(u_send.at[g], u_s.at[g])
        pltpu.make_async_copy(g_send.at[g, pl.ds(0, 3)], g_send.at[g, pl.ds(0, 3)], g_s.at[g]).wait()


def local(tokens, w_in, short_taps, skip_bias, filter_spectra, w_out):
    inner_table, first_table, last_table, twist, pick = tables()
    vmem = pl.BlockSpec(memory_space=pltpu.VMEM)
    hbm = pl.BlockSpec(memory_space=pltpu.HBM)
    dma = pltpu.SemaphoreType.DMA
    return pl.pallas_call(
        body,
        out_shape=jax.ShapeDtypeStruct((OUT_ROWS, 1024), BF),
        in_specs=[hbm] * 11,
        out_specs=vmem,
        scratch_shapes=[
            pltpu.SMEM((3, 3, CH), F32),
            pltpu.SMEM((2, CH), F32),
            pltpu.VMEM((3, 3, CH), F32),
            pltpu.VMEM((2 * RES, 3 * SEQ), BF),
            pltpu.VMEM((SEQ, 6 * RES), BF),
            pltpu.VMEM((2, RES, ROWS), F32),
            pltpu.VMEM((512, 512), BF),
            pltpu.VMEM((2, 2, 2, ROWS, CH), F32),
            pltpu.VMEM((3, 1024, CH), BF),
            pltpu.VMEM((4, ROWS, ROWS), BF),
            pltpu.VMEM((2, 2 * ROWS, 2 * ROWS), BF),
            pltpu.VMEM((TP, OUT_ROWS, 1024), BF),
            pltpu.VMEM((TP, 2, 128, 1024), BF),
            pltpu.VMEM((4, SEQ, 8, ROWS), BF),
            pltpu.VMEM((4, SEQ, 8, ROWS), BF),
            pltpu.VMEM((SEQ, 8, ROWS), BF),
            pltpu.VMEM((SEQ, 8, ROWS), BF),
            pltpu.VMEM((2, SEQ, 2, ROWS), BF),
            pltpu.VMEM((2, SEQ, 2, ROWS), BF),
            pltpu.VMEM((SEQ, 8, ROWS), F32),
            pltpu.VMEM((ROWS, CH), BF),
            pltpu.VMEM((16, CH), BF),
            pltpu.VMEM((ROWS, CH), F32),
            pltpu.VMEM((2, TP, OUT_ROWS, 128), BF),
            pltpu.VMEM((2, TP, OUT_ROWS, 128), BF),
            dma((13,)),
            dma((12,)),
            dma, dma, dma, dma,
            dma((4,)),
            dma((4,)),
            dma, dma, dma, dma, dma((2,)), dma((2,)), dma((2,)), dma((2,)),
        ],
        compiler_params=pltpu.CompilerParams(
            collective_id=0, has_side_effects=True, vmem_limit_bytes=40 * 1024 * 1024
        ),
    )(
        *[pltpu.with_memory_space_constraint(item, pltpu.HBM) for item in (
        tokens, w_in, short_taps, skip_bias, filter_spectra, w_out.reshape(2, 128, 1024),
        jnp.asarray(inner_table), jnp.asarray(first_table), jnp.asarray(last_table),
        jnp.asarray(twist), jnp.asarray(pick),
            )]
    )


def solution(mesh):
    in_specs = (
        P(("seq", "tp"), None),
        P(None, None, "tp"),
        P(None, None, "tp"),
        P(None, "tp"),
        P(None, None, "seq", None, "tp"),
        P("tp", None),
    )
    out_specs = P(("seq", "tp"), None)
    return jax.shard_map(local, mesh=mesh, in_specs=in_specs, out_specs=out_specs, check_vma=False)
```

```python
import math

import jax
import jax.numpy as jnp
import ml_dtypes
import numpy as np
from jax import lax
from jax.experimental import pallas as pl
from jax.experimental.pallas import tpu as pltpu
from jax.sharding import PartitionSpec as P

MESH = pl.DeviceIdType.MESH
BF = jnp.bfloat16
F32 = jnp.float32
SEQ, TP = 64, 4
ROWS, CH, OUT_ROWS = 384, 256, 96
RES = 128
NT = (((1,), (1,)), ((), ()))
NN = (((1,), (0,)), ((), ()))


def halves(table):
    high = table.astype(ml_dtypes.bfloat16)
    low = (table - high.astype(np.float64)).astype(ml_dtypes.bfloat16)
    return high, low


def tables():
    total = RES * ROWS
    line = np.arange(ROWS)
    inner = 2.0 * np.pi / ROWS * (np.outer(line, line) % ROWS)
    cos_hi, cos_lo = halves(np.cos(inner))
    sin_hi, sin_lo = halves(np.sin(inner))
    inner_table = np.stack([cos_hi, sin_hi, cos_lo, sin_lo])
    order = np.concatenate([2 * np.arange(SEQ), 2 * np.arange(SEQ) + 1])
    outer = 2.0 * np.pi / RES * (np.outer(order, np.arange(SEQ)) % RES)
    first = np.concatenate([np.cos(outer), -np.sin(outer)], axis=0)
    first_hi, first_lo = halves(first)
    first_table = np.concatenate([first_hi, first_hi, first_lo], axis=1)
    last = np.concatenate([np.cos(outer.T), -np.sin(outer.T)], axis=1) / total
    last_hi, last_lo = halves(last)
    last_table = np.concatenate([last_hi, last_hi, last_lo], axis=1)
    angle = -2.0 * np.pi / total * np.outer(order, line)
    twist = np.stack([np.cos(angle), np.sin(angle)]).astype(np.float32)
    pick = np.zeros((512, 512), ml_dtypes.bfloat16)
    for dest in range(SEQ):
        for slot in range(4):
            for low in range(2):
                pick[dest * 8 + slot * 2 + low, slot * 128 + low * 64 + dest] = 1
    return inner_table, first_table, last_table, twist, pick


def split(value):
    high = value.astype(BF)
    low = (value - high.astype(F32)).astype(BF)
    return high, low


def dot(a, b, dims=NN):
    return lax.dot_general(a, b, dims, preferred_element_type=F32)


def body(
    tok, w_in, taps_h, bias_h, spec, w_out, inner_h, first_h, last_h, twist_h, pick_h,
    out,
    taps_s, bias_s, taps_v, first_c, last_c, twist_c, pick_c, spec_v, w_in_v, inner_v, wmat, tg, wg, h_send, h_recv, f_send, f_recv, u_send, u_recv,
    wide, f2_v, halo, gate_v, g_send, g_recv,
    load_sem, own_sem, tok_s, tok_r, wo_s, wo_r, h_s, h_r, f_s, f_r, halo_s, halo_r, u_s, u_r, g_s, g_r,
):
    me = lax.axis_index("seq")
    mx = lax.axis_index("tp")

    def peer(i):
        to = me + i
        return jnp.where(to >= SEQ, to - SEQ, to)

    barrier = pltpu.get_barrier_semaphore()

    def greet(i, carry):
        pl.semaphore_signal(barrier, inc=1, device_id={"seq": peer(i)}, device_id_type=MESH)
        return carry

    lax.fori_loop(1, SEQ, greet, 0, unroll=63)
    for t in range(1, TP):
        pl.semaphore_signal(barrier, inc=1, device_id={"tp": (mx + t) % TP}, device_id_type=MESH)

    def half(ref, o, g):
        return ref.at[o, :, :, :, pl.ds(128 * g, 128)]

    def loads(k):
        pairs = (
            (half(spec, 0, 0), half(spec_v, 0, 0)), (pick_h, pick_c), (half(spec, 0, 1), half(spec_v, 0, 1)),
            (w_in, w_in_v), (half(spec, 1, 0), half(spec_v, 1, 0)), (half(spec, 1, 1), half(spec_v, 1, 1)),
            (inner_h, inner_v), (first_h, first_c), (twist_h, twist_c), (last_h, last_c),
            (taps_h, taps_v), (taps_h, taps_s), (bias_h, bias_s),
        )
        return pltpu.make_async_copy(pairs[k][0], pairs[k][1], load_sem.at[k])

    for k in range(13):
        loads(k).start()

    def x_copy(src, dst, ssem, rsem, t):
        return pltpu.make_async_remote_copy(
            src, dst, ssem, rsem, device_id={"tp": (mx + t) % TP}, device_id_type=MESH
        )

    def own_copy(src, dst, k):
        return pltpu.make_async_copy(src, dst, own_sem.at[k])

    def all_wait(src_slice, dst_slice, ssem, rsem):
        pltpu.make_async_copy(src_slice, src_slice, ssem).wait()
        pltpu.make_async_copy(dst_slice, dst_slice, rsem).wait()

    def spread(send, recv, ssem, rsem, k):
        def one(i, carry):
            to = peer(i)
            pltpu.make_async_remote_copy(
                send.at[to], recv.at[me], ssem, rsem, device_id={"seq": to}, device_id_type=MESH
            ).start()
            return carry

        lax.fori_loop(1, SEQ, one, 0, unroll=63 if k >= 8 else 7)
        own_copy(send.at[me], recv.at[me], k).start()

    def gathered(send, recv, ssem, rsem, k):
        own_copy(send.at[me], recv.at[me], k).wait()
        pltpu.make_async_copy(recv.at[pl.ds(0, SEQ - 1)], recv.at[pl.ds(0, SEQ - 1)], rsem).wait()

    def sent(send, ssem):
        pltpu.make_async_copy(send.at[pl.ds(0, SEQ - 1)], send.at[pl.ds(0, SEQ - 1)], ssem).wait()

    def turn_filter(o, g):
        k = 2 * o + g
        lanes = slice(128 * g, 128 * g + 128)
        line = jnp.concatenate(
            [spec_v[o, ri, j, :, lanes].astype(BF) for ri in range(2) for j in range(2)], axis=1
        )
        turned = dot(pick_c[...], line, NT)
        h_send[k] = turned.reshape(SEQ, 8, ROWS).astype(BF)

    def ship_filter(k):
        spread(h_send.at[k], h_recv.at[k], h_s.at[k], h_r.at[k], 4 + k)

    loads(0).wait()
    loads(1).wait()
    turn_filter(0, 0)
    pl.semaphore_wait(barrier, SEQ - 1 + TP - 1)
    for t in range(1, TP):
        x_copy(tok, tg.at[mx], tok_s, tok_r, t).start()
    own_copy(tok, tg.at[mx], 0).start()
    ship_filter(0)
    loads(2).wait()
    turn_filter(0, 1)
    ship_filter(1)

    for t in range(1, TP):
        x_copy(w_out, wg.at[mx], wo_s, wo_r, t).start()
    own_copy(w_out, wg.at[mx], 1).start()

    loads(3).wait()
    own_copy(tok, tg.at[mx], 0).wait()
    pltpu.make_async_copy(tg.at[pl.ds(0, 3)], tg.at[pl.ds(0, 3)], tok_r).wait()
    rows = tg[...].reshape(ROWS, 1024)
    lines = [dot(rows, w_in_v[b]).astype(BF) for b in range(3)]
    turned = dot(pick_c[...], jnp.concatenate(lines[:2], axis=1), NT)
    f_send[...] = turned.reshape(SEQ, 8, ROWS).astype(BF)
    spread(f_send, f_recv, f_s, f_r, 2)
    f2_v[...] = lines[2]
    after = (me + 1) % SEQ
    edge = pltpu.make_async_remote_copy(
        f2_v.at[pl.ds(ROWS - 16, 16)], halo, halo_s, halo_r, device_id={"seq": after}, device_id_type=MESH
    )
    edge.start()

    for g in range(2):
        loads(4 + g).wait()
        turn_filter(1, g)
        ship_filter(2 + g)

    for k in range(6, 13):
        loads(k).wait()
    for part in range(2):
        cos_t = inner_v[2 * part]
        sin_t = inner_v[2 * part + 1]
        wmat[part, 0:ROWS, 0:ROWS] = cos_t
        wmat[part, ROWS:, ROWS:] = cos_t
        wmat[part, ROWS:, 0:ROWS] = sin_t
        wmat[part, 0:ROWS, ROWS:] = -sin_t

    def thrice(value, dims):
        high, low = split(value)
        return dot(high, wmat[0], dims) + dot(low, wmat[0], dims) + dot(high, wmat[1], dims)

    def stacked(value):
        high, low = split(value)
        return jnp.concatenate([high, low, high], axis=0)

    tr, ti = twist_c[0], twist_c[1]

    def forward(pair):
        z = dot(first_c[...], stacked(jnp.concatenate(pair, axis=1)))
        blocks = []
        for low in range(2):
            cols = slice(ROWS * low, ROWS * low + ROWS)
            zr, zi = z[:RES, cols], z[RES:, cols]
            blocks.append(jnp.concatenate([zr * tr - zi * ti, zr * ti + zi * tr], axis=1))
        return thrice(jnp.concatenate(blocks, axis=0), NN)

    def inverse(x, k):
        gathered(h_send.at[k], h_recv.at[k], h_s.at[k], h_r.at[k], 4 + k)
        wide[...] = h_recv[k].astype(F32)
        blocks = []
        for low in range(2):
            for j in range(2):
                at = low * RES + j * SEQ
                xr, xi = x[at : at + SEQ, :ROWS], x[at : at + SEQ, ROWS:]
                hr = wide[:, j * 2 + low, :]
                hi = wide[:, (2 + j) * 2 + low, :]
                blocks.append(jnp.concatenate([xr * hr - xi * hi, xr * hi + xi * hr], axis=1))
        lines_in = jnp.concatenate(blocks, axis=0)
        v = thrice(lines_in, NT) if k < 2 else dot(lines_in.astype(BF), wmat[0], NT)
        real, imag = [], []
        for low in range(2):
            vr, vi = v[RES * low : RES * low + RES, :ROWS], v[RES * low : RES * low + RES, ROWS:]
            real.append(vr * tr + vi * ti)
            imag.append(vi * tr - vr * ti)
        rhs = jnp.concatenate([jnp.concatenate(real, axis=1), jnp.concatenate(imag, axis=1)], axis=0)
        y = dot(last_c[...], stacked(rhs)) if k < 2 else dot(last_c[:, : 2 * RES], rhs.astype(BF))
        return [y[:, :ROWS], y[:, ROWS:]]

    at_row = lax.broadcasted_iota(jnp.int32, (SEQ, ROWS), 0)
    at_col = lax.broadcasted_iota(jnp.int32, (SEQ, ROWS), 1)

    def delayed(x, by):
        turned = pltpu.roll(x, by, 1)
        fix = jnp.where(at_row == 0, 0.0, pltpu.roll(turned, 1, 0))
        return jnp.where(at_col < by, fix, turned)

    def filtered(b, i):
        x = wide[:, b * 4 + i, :]
        col = 64 * i + me
        return taps_s[b, 0, col] * x + taps_s[b, 1, col] * delayed(x, 1) + taps_s[b, 2, col] * delayed(x, 2)

    gathered(f_send, f_recv, f_s, f_r, 2)
    wide[...] = f_recv[...].astype(F32)
    values = [filtered(0, i) for i in range(4)]
    gates = [filtered(1, i) for i in range(4)]
    spectra = [forward(values[2 * g : 2 * g + 2]) for g in range(2)]
    carried = []
    for g in range(2):
        ys = inverse(spectra[g], g)
        for low in range(2):
            i = 2 * g + low
            carried.append(gates[i] * (ys[low] + bias_s[0, 64 * i + me] * values[i]))
        spectra[g] = forward(carried[2 * g : 2 * g + 2])

    edge.wait()
    x = f2_v[...].astype(F32)
    edge_rows = jnp.where(me > 0, halo[...].astype(F32), 0.0)
    at = lax.broadcasted_iota(jnp.int32, (ROWS, CH), 0)
    one = jnp.where(at == 0, edge_rows[15:16], pltpu.roll(x, 1, 0))
    two = jnp.where(at == 0, edge_rows[14:15], jnp.where(at == 1, edge_rows[15:16], pltpu.roll(x, 2, 0)))
    gate_v[...] = taps_v[2, 0:1, :] * x + taps_v[2, 1:2, :] * one + taps_v[2, 2:3, :] * two

    for g in range(2):
        ys = inverse(spectra[g], 2 + g)
        for low in range(2):
            i = 2 * g + low
            wide[:, low, :] = ys[low] + bias_s[1, 64 * i + me] * carried[i]
        u_send[g] = wide[:, 0:2, :].astype(BF)
        spread(u_send.at[g], u_recv.at[g], u_s.at[g], u_r.at[g], 8 + g)

    for g in range(2):
        gathered(u_send.at[g], u_recv.at[g], u_s.at[g], u_r.at[g], 8 + g)
        wide[:, 0:2, :] = u_recv[g].astype(F32)
        turned = jnp.concatenate([wide[:, low, :] for low in range(2)], axis=0).T
        lanes = slice(128 * g, 128 * g + 128)
        g_send[g] = (gate_v[:, lanes] * turned).astype(BF).reshape(TP, OUT_ROWS, 128)
        for t in (2, 1, 3):
            x_copy(g_send.at[g, (mx + t) % TP], g_recv.at[g, mx], g_s.at[g], g_r.at[g], t).start()
        own_copy(g_send.at[g, mx], g_recv.at[g, mx], 10 + g).start()
    own_copy(w_out, wg.at[mx], 1).wait()
    pltpu.make_async_copy(wg.at[pl.ds(0, 3)], wg.at[pl.ds(0, 3)], wo_r).wait()
    parts = []
    for g in range(2):
        own_copy(g_send.at[g, mx], g_recv.at[g, mx], 10 + g).wait()
        pltpu.make_async_copy(g_recv.at[g, pl.ds(0, 3)], g_recv.at[g, pl.ds(0, 3)], g_r.at[g]).wait()
        line = jnp.concatenate([g_recv[g, t] for t in range(TP)], axis=1)
        parts.append(dot(line, wg[:, g].reshape(512, 1024)))
    out[...] = (parts[0] + parts[1]).astype(BF)

    pltpu.make_async_copy(tg.at[pl.ds(0, 3)], tg.at[pl.ds(0, 3)], tok_s).wait()
    pltpu.make_async_copy(wg.at[pl.ds(0, 3)], wg.at[pl.ds(0, 3)], wo_s).wait()
    for k in range(4):
        sent(h_send.at[k], h_s.at[k])
    sent(f_send, f_s)
    for g in range(2):
        sent(u_send.at[g], u_s.at[g])
        pltpu.make_async_copy(g_send.at[g, pl.ds(0, 3)], g_send.at[g, pl.ds(0, 3)], g_s.at[g]).wait()


def local(tokens, w_in, short_taps, skip_bias, filter_spectra, w_out):
    inner_table, first_table, last_table, twist, pick = tables()
    vmem = pl.BlockSpec(memory_space=pltpu.VMEM)
    hbm = pl.BlockSpec(memory_space=pltpu.HBM)
    dma = pltpu.SemaphoreType.DMA
    return pl.pallas_call(
        body,
        out_shape=jax.ShapeDtypeStruct((OUT_ROWS, 1024), BF),
        in_specs=[hbm] * 11,
        out_specs=vmem,
        scratch_shapes=[
            pltpu.SMEM((3, 3, CH), F32),
            pltpu.SMEM((2, CH), F32),
            pltpu.VMEM((3, 3, CH), F32),
            pltpu.VMEM((2 * RES, 3 * SEQ), BF),
            pltpu.VMEM((SEQ, 6 * RES), BF),
            pltpu.VMEM((2, RES, ROWS), F32),
            pltpu.VMEM((512, 512), BF),
            pltpu.VMEM((2, 2, 2, ROWS, CH), F32),
            pltpu.VMEM((3, 1024, CH), BF),
            pltpu.VMEM((4, ROWS, ROWS), BF),
            pltpu.VMEM((2, 2 * ROWS, 2 * ROWS), BF),
            pltpu.VMEM((TP, OUT_ROWS, 1024), BF),
            pltpu.VMEM((TP, 2, 128, 1024), BF),
            pltpu.VMEM((4, SEQ, 8, ROWS), BF),
            pltpu.VMEM((4, SEQ, 8, ROWS), BF),
            pltpu.VMEM((SEQ, 8, ROWS), BF),
            pltpu.VMEM((SEQ, 8, ROWS), BF),
            pltpu.VMEM((2, SEQ, 2, ROWS), BF),
            pltpu.VMEM((2, SEQ, 2, ROWS), BF),
            pltpu.VMEM((SEQ, 8, ROWS), F32),
            pltpu.VMEM((ROWS, CH), BF),
            pltpu.VMEM((16, CH), BF),
            pltpu.VMEM((ROWS, CH), F32),
            pltpu.VMEM((2, TP, OUT_ROWS, 128), BF),
            pltpu.VMEM((2, TP, OUT_ROWS, 128), BF),
            dma((13,)),
            dma((12,)),
            dma, dma, dma, dma,
            dma((4,)),
            dma((4,)),
            dma, dma, dma, dma, dma((2,)), dma((2,)), dma((2,)), dma((2,)),
        ],
        compiler_params=pltpu.CompilerParams(
            collective_id=0, has_side_effects=True, vmem_limit_bytes=40 * 1024 * 1024
        ),
    )(
        *[pltpu.with_memory_space_constraint(item, pltpu.HBM) for item in (
        tokens, w_in, short_taps, skip_bias, filter_spectra, w_out.reshape(2, 128, 1024),
        jnp.asarray(inner_table), jnp.asarray(first_table), jnp.asarray(last_table),
        jnp.asarray(twist), jnp.asarray(pick),
            )]
    )


def solution(mesh):
    in_specs = (
        P(("seq", "tp"), None),
        P(None, None, "tp"),
        P(None, None, "tp"),
        P(None, "tp"),
        P(None, None, "seq", None, "tp"),
        P("tp", None),
    )
    out_specs = P(("seq", "tp"), None)
    return jax.shard_map(local, mesh=mesh, in_specs=in_specs, out_specs=out_specs, check_vma=False)
```
